256 devices in a mesh: seq: 64 (over y, z, core), mp: 4 (over x).
Axes of the slice: x: 4, y: 4, z: 8, core: 2. Of those that a mesh axis runs over, the one named last changes fastest.
Arguments:
- byte_acts: bfloat16 [32768, 2048], P('seq', 'mp'), may hold values from -20 to 20
- byte_grads: bfloat16 [32768, 2048], P('seq', 'mp'), may hold values from -6 to 6
- row_of_byte: int32 [32768], P('seq'), may hold values from 0 to 14239, as said below
- w_in: bfloat16 [2048, 4096], P('seq', 'mp'), may hold values from -0.125 to 0.125
- w_out: bfloat16 [2048, 4096], P('seq', 'mp'), may hold values from -0.09375 to 0.09375
Outputs:
- byte_act_grad: bfloat16 [32768, 2048], P('seq', 'mp')
- grad_in: float32 [2048, 4096], P('seq', 'mp')
- grad_out: float32 [2048, 4096], P('seq', 'mp')
The draws below stay inside these ranges and needn't reach their ends.
Inputs may be any that keep to these rules, and one draw needn't show every extreme that they name: `row_of_byte`: equal values form runs of bytes, the segments, and values never fall along the sequence; the first byte begins a segment. With shards of 512 bytes, the j-th segment that begins in shard k has the value k * 224 + j, and between 32 and 224 segments begin in each shard, 224 in some shard and 128 in the last one. The segments that begin in shards 0 to k - 1 number k * 128 plus 0 to 3 * 128 // 4 (both ends are reached), and 8192 in all.
All inputs are finite; a program needn't handle non-finite values.
Results may differ from the reference program's by a relative error of at most 0.0075.
Values may be sent and summed in bfloat16 or wider, within the bound.
No kernel may reach another device: no remote copies, remote signals or barrier semaphores. Data moves between devices by JAX's collectives and lax.ppermute only.
A program may use at most 64 MiB of HBM per device.

```python
import math
import jax
import jax.numpy as jnp
from jax import lax

D = 2048
FF = 4096
BYTES_DEV = 512
BAL = 128
CAP = 224
SHARDS = 64
SEQ_LEN = 32768


def draw_byte_acts(key, part):
    key_val, key_col = jax.random.split(key, 2)
    columns = 10.0 ** jax.random.uniform(key_col, (1, D), jnp.float32, -0.5, 0.5)
    values = jnp.clip(jax.random.normal(key_val, (SEQ_LEN, D), jnp.float32), -5.0, 5.0)
    return (values * columns).astype(jnp.bfloat16)


def draw_row_of_byte(key, part):
    shards = SEQ_LEN // BYTES_DEV
    spread = 3 * BAL // 4
    key_drift, key_full, key_pick = jax.random.split(key, 3)
    shard_ids = jnp.arange(shards, dtype=jnp.int32)
    drifts = jax.random.randint(key_drift, (shards,), 0, spread + 1)
    full_shard = jax.random.randint(key_full, (), 1, shards - 2)
    drifts = jnp.where(shard_ids == full_shard, spread, drifts)
    drifts = jnp.where(shard_ids == full_shard - 1, 0, drifts)
    drifts = jnp.where(shard_ids == shards - 2, 0, drifts)
    drifts = jnp.where(shard_ids == shards - 1, 0, drifts)
    before = jnp.concatenate([jnp.zeros((1,), jnp.int32), drifts[:-1]])
    counts = (BAL + drifts - before).astype(jnp.int32)
    scores = jax.random.randint(key_pick, (shards, BYTES_DEV), 0, 2 ** 18) * BYTES_DEV
    scores = scores + jnp.arange(BYTES_DEV, dtype=jnp.int32)[None, :]
    scores = scores.at[0, 0].set(-1)
    order_idx = jnp.argsort(scores, axis=1)
    rank_of = jnp.argsort(order_idx, axis=1)
    starts = (rank_of < counts[:, None]).astype(jnp.int32)
    local_slot = jnp.cumsum(starts, axis=1) - 1
    prev_counts = jnp.concatenate([jnp.zeros((1,), jnp.int32), counts[:-1]])
    rows_here = shard_ids[:, None] * CAP + local_slot
    rows_prev = (shard_ids[:, None] - 1) * CAP + prev_counts[:, None] - 1
    return jnp.where(local_slot >= 0, rows_here, rows_prev).reshape(-1).astype(jnp.int32)


def level_of(rng, dims, cuts, least, high):
    gain, own = 1.0, jax.random.fold_in(rng, 6)
    for axis_at, parts in cuts:
        draws = jnp.exp(jax.random.uniform(jax.random.fold_in(own, axis_at), (parts,), jnp.float32, least / len(cuts), high / len(cuts)))
        gain = gain * jnp.repeat(draws, dims[axis_at] // parts).reshape([-1 if axis == axis_at else 1 for axis in range(len(dims))])
    return gain


def noise(rng, extent, scale, most, cuts=(), held_as=jnp.bfloat16):
    gain = level_of(rng, extent, cuts, -0.22, 0.18) if cuts else 1.0
    drawn = jax.random.normal(rng, extent, jnp.float32) * scale * gain
    return jnp.minimum(jnp.maximum(drawn, -most), most).astype(held_as)


def setup_inputs(seed: int = 0) -> dict:
    splits = jax.random.split(jax.random.key(seed), 6)
    byte_acts = draw_byte_acts(jax.random.fold_in(splits[5], 71), 0)
    byte_grads = noise(splits[1], (SEQ_LEN, D), 1.0, 6.0, ((0, 64), (1, 4)))
    row_of_byte = draw_row_of_byte(jax.random.fold_in(splits[5], 71), 0)
    w_in = noise(splits[3], (D, FF), D ** -0.5, 0.125, ((0, 64), (1, 4)))
    w_out = noise(splits[4], (D, FF), FF ** -0.5, 0.09375, ((0, 64), (1, 4)))
    return dict(byte_acts=byte_acts, byte_grads=byte_grads, row_of_byte=row_of_byte, w_in=w_in, w_out=w_out)


epsilon = 1e-05

def gelu_tanh(values):
    return jax.nn.gelu(values, approximate=True)

def reference(byte_acts, byte_grads, row_of_byte, w_in, w_out):
    total_rows = SHARDS * CAP
    byte_ones = jnp.ones(row_of_byte.shape, jnp.float32)
    row_lengths = jax.ops.segment_sum(byte_ones, row_of_byte, num_segments=total_rows)
    inv_length = 1.0 / jnp.maximum(row_lengths, 1.0)
    act_sums = jax.ops.segment_sum(byte_acts.astype(jnp.float32), row_of_byte, num_segments=total_rows)
    pooled_all = (act_sums * inv_length[:, None]).astype(jnp.bfloat16)
    up_all = jax.ops.segment_sum(byte_grads.astype(jnp.float32), row_of_byte, num_segments=total_rows).astype(jnp.bfloat16)
    live_rows = jnp.nonzero(row_lengths > 0, size=SHARDS * BAL)[0].astype(jnp.int32)
    pooled = pooled_all[live_rows]
    up_grad = up_all[live_rows]
    pooled_f32 = pooled.astype(jnp.float32)
    inv_rms = lax.rsqrt(lax.optimization_barrier(jnp.mean(pooled_f32 * pooled_f32, axis=1)) + epsilon)
    normed = (pooled_f32 * inv_rms[:, None]).astype(jnp.bfloat16)
    pre_act = jnp.dot(normed, w_in, preferred_element_type=jnp.float32)
    activation = gelu_tanh(pre_act).astype(jnp.bfloat16)
    up_proj = jnp.dot(up_grad, w_out, preferred_element_type=jnp.float32)
    act_grad = jax.vjp(gelu_tanh, pre_act)[1](up_proj)[0].astype(jnp.bfloat16)
    normed_grad = lax.dot_general(act_grad, w_in, (((1,), (1,)), ((), ())), preferred_element_type=jnp.float32)
    row_stat = lax.optimization_barrier(jnp.mean(normed_grad * pooled_f32, axis=1))
    pooled_grad = (up_grad.astype(jnp.float32) + inv_rms[:, None] * normed_grad - pooled_f32 * (inv_rms ** 3 * row_stat)[:, None]).astype(jnp.bfloat16)
    grad_scale = 1.0 / math.sqrt(SHARDS * BAL)
    grad_in = lax.dot_general(normed, act_grad, (((0,), (0,)), ((), ())), preferred_element_type=jnp.float32) * grad_scale
    grad_out = lax.dot_general(up_grad, activation, (((0,), (0,)), ((), ())), preferred_element_type=jnp.float32) * grad_scale
    grad_rows = jnp.zeros((total_rows, D), jnp.bfloat16).at[live_rows].set(pooled_grad)
    spread_grad = grad_rows[row_of_byte].astype(jnp.float32) * inv_length[row_of_byte][:, None]
    byte_act_grad = (byte_grads.astype(jnp.float32) + spread_grad).astype(jnp.bfloat16)
    return (byte_act_grad, grad_in, grad_out)
```

```python
import math

import jax
import jax.numpy as jnp
from jax import lax
from jax.sharding import PartitionSpec as P

BAL = 128
CAP = 224
NY, NZ, NC, NX = 4, 8, 2, 4
SEQ = NY * NZ * NC
epsilon = 1e-05
bf16 = jnp.bfloat16
f32 = jnp.float32


def seq_of(y, z, c):
    return ((y % NY) * NZ + (z % NZ)) * NC + c


def coords_of(s):
    return s // (NZ * NC), (s // NC) % NZ, s % NC


CORE_SWAP = [(s, s ^ 1) for s in range(SEQ)]
Z_GROUPS = [[seq_of(y, z, c) for z in range(NZ)] for y in range(NY) for c in range(NC)]


def y_pairs(step):
    pairs = []
    for s in range(SEQ):
        y, z, c = coords_of(s)
        pairs.append((s, seq_of(y + step, z, c)))
    return pairs


def swap_cores(value):
    return lax.ppermute(value, "seq", CORE_SWAP)


def send_y(value, step):
    return lax.ppermute(value, "seq", y_pairs(step))


def send_x(value, step):
    return lax.ppermute(value, "mp", [(i, (i + step) % NX) for i in range(NX)])


def z_exchange(value):
    return lax.all_to_all(value, "seq", 0, 0, axis_index_groups=Z_GROUPS, tiled=True)


def pick(value, index):
    return lax.dynamic_index_in_dim(value, index, 0, keepdims=False)


def gelu_tanh(values):
    return jax.nn.gelu(values, approximate=True)


def by_core(core, own, other, axis):
    first = jnp.where(core == 0, own, other)
    second = jnp.where(core == 0, other, own)
    return jnp.concatenate([first, second], axis=axis)


def gather_weight(part, y_idx):
    copies = jnp.broadcast_to(part[None], (NZ,) + part.shape)
    column = z_exchange(copies).reshape(1, NZ * part.shape[0], part.shape[1])
    full = jnp.zeros((NY,) + column.shape[1:], column.dtype)
    full = lax.dynamic_update_slice_in_dim(full, column, y_idx, 0)
    for step in (1, 3, 2):
        full = lax.dynamic_update_slice_in_dim(
            full, send_y(column, step), (y_idx - step) % NY, 0
        )
    return full


def y_reduce(pieces, y_idx):
    total = pick(pieces, y_idx)
    for step in (1, 3, 2):
        got = send_y(pick(pieces, (y_idx + step) % NY).astype(bf16), step)
        total = total + got.astype(f32)
    return total


def z_reduce(pieces):
    return jnp.sum(z_exchange(pieces.astype(bf16)).astype(f32), axis=0)


def local(byte_acts, byte_grads, row_of_byte, w_in, w_out):
    quarter = byte_acts.shape[1]
    width = quarter * NX
    hidden = w_in.shape[1] // NC
    shard_idx = lax.axis_index("seq")
    x_idx = lax.axis_index("mp")
    core, y_idx = shard_idx % NC, shard_idx // (NZ * NC)

    both = jnp.stack([w_in, w_out])
    halves = both.reshape(2, both.shape[1], NC, hidden)
    keep = lax.dynamic_index_in_dim(halves, core, 2, keepdims=False)
    give = lax.dynamic_index_in_dim(halves, 1 - core, 2, keepdims=False)
    chip_rows = by_core(core, keep, swap_cores(give), 1)
    full_w_in = gather_weight(chip_rows[0], y_idx).reshape(width, hidden)
    full_w_out = gather_weight(chip_rows[1], y_idx).reshape(width, hidden)

    local_row = row_of_byte - shard_idx * CAP
    leading = local_row < 0
    slot_idx = jnp.where(leading, CAP, local_row)
    one_hot = (jnp.arange(CAP + 1, dtype=jnp.int32)[:, None] == slot_idx[None, :]).astype(bf16)
    act_sums = jnp.dot(one_hot, byte_acts, preferred_element_type=f32)
    grad_sums = jnp.dot(one_hot, byte_grads, preferred_element_type=f32)
    byte_counts = jnp.sum(one_hot.astype(f32), axis=1)
    own_count = jnp.max(jnp.where(leading, -1, local_row)) + 1
    frag = jnp.stack(
        [act_sums[CAP], grad_sums[CAP], jnp.broadcast_to(byte_counts[CAP], (quarter,))]
    )
    frag = lax.ppermute(frag, "seq", [(s, s - 1) for s in range(1, SEQ)])
    last_mark = (jnp.arange(CAP, dtype=jnp.int32) == own_count - 1).astype(f32)
    act_total = act_sums[:CAP] + last_mark[:, None] * frag[0][None, :]
    grad_total = grad_sums[:CAP] + last_mark[:, None] * frag[1][None, :]
    row_lengths = byte_counts[:CAP] + last_mark * frag[2, 0]
    inv_length = 1.0 / jnp.maximum(row_lengths, 1.0)
    pooled = (act_total * inv_length[:, None]).astype(bf16)
    up_grad = grad_total.astype(bf16)

    rows = jnp.stack([pooled, up_grad])
    wide = jnp.zeros((2, CAP, width), bf16)
    wide = lax.dynamic_update_slice_in_dim(wide, rows, x_idx * quarter, 2)
    for step in (1, 3, 2):
        wide = lax.dynamic_update_slice_in_dim(
            wide, send_x(rows, step), ((x_idx - step) % NX) * quarter, 2
        )
    wide = jnp.concatenate([wide, swap_cores(wide)], axis=1)
    wide_pooled, wide_up = wide[0], wide[1]

    wide_f32 = wide_pooled.astype(f32)
    inv_rms = lax.rsqrt(jnp.mean(wide_f32 * wide_f32, axis=1) + epsilon)
    normed = (wide_f32 * inv_rms[:, None]).astype(bf16)
    pre_act = jnp.dot(normed, full_w_in, preferred_element_type=f32)
    activation = gelu_tanh(pre_act).astype(bf16)
    out_part = lax.dot_general(
        wide_up, activation, (((0,), (0,)), ((), ())), preferred_element_type=f32
    )
    out_rows = z_reduce(
        out_part.astype(bf16).reshape(NY, NZ, NC * 32, hidden).transpose(1, 0, 2, 3)
    )
    grad_out = y_reduce(out_rows, y_idx)

    up_proj = jnp.dot(wide_up, full_w_out, preferred_element_type=f32)
    act_grad = jax.vjp(gelu_tanh, pre_act)[1](up_proj)[0].astype(bf16)
    in_part = lax.dot_general(
        normed, act_grad, (((0,), (0,)), ((), ())), preferred_element_type=f32
    )
    in_rows = y_reduce(in_part.reshape(NY, NZ * NC * 32, hidden), y_idx)
    grad_in = z_reduce(in_rows.reshape(NZ, NC * 32, hidden))

    normed_part = lax.dot_general(
        act_grad, full_w_in, (((1,), (1,)), ((), ())), preferred_element_type=f32
    )
    stat_part = jnp.sum(act_grad.astype(f32) * pre_act, axis=1) / inv_rms
    stat_high = stat_part.astype(bf16)
    stat_low = (stat_part - stat_high.astype(f32)).astype(bf16)
    lane = jnp.arange(128)[None, :]
    stat_cols = jnp.where(lane == 0, stat_high[:, None], stat_low[:, None])
    stat_cols = jnp.where(lane < 2, stat_cols, jnp.zeros((), bf16))
    sent = jnp.concatenate([normed_part[CAP:].astype(bf16), stat_cols[CAP:]], axis=1)
    got = swap_cores(sent).astype(f32)
    chip_part = normed_part[:CAP] + got[:, :width]
    chip_stat = stat_part[:CAP] + got[:, width] + got[:, width + 1]
    stat_high = chip_stat.astype(bf16)
    stat_low = (chip_stat - stat_high.astype(f32)).astype(bf16)
    stat_cols = jnp.where(lane == 0, stat_high[:, None], stat_low[:, None])
    stat_cols = jnp.where(lane < 2, stat_cols, jnp.zeros((), bf16))
    normed_grad = lax.dynamic_slice_in_dim(chip_part, x_idx * quarter, quarter, 1)
    row_stat = chip_stat
    for step in (1, 3, 2):
        piece = lax.dynamic_slice_in_dim(
            chip_part, ((x_idx + step) % NX) * quarter, quarter, 1
        ).astype(bf16)
        got = send_x(jnp.concatenate([piece, stat_cols], axis=1), step).astype(f32)
        normed_grad = normed_grad + got[:, :quarter]
        row_stat = row_stat + got[:, quarter] + got[:, quarter + 1]
    row_stat = row_stat / width
    own_rms = inv_rms[:CAP]
    pooled_grad = (
        up_grad.astype(f32)
        + own_rms[:, None] * normed_grad
        - pooled.astype(f32) * (own_rms**3 * row_stat)[:, None]
    ).astype(bf16)

    grad_spread = pooled_grad.astype(f32) * inv_length[:, None]
    last_spread = lax.dynamic_slice_in_dim(grad_spread, own_count - 1, 1, 0)
    tail_spread = lax.ppermute(last_spread, "seq", [(s, s + 1) for s in range(SEQ - 1)])
    grad_table = jnp.concatenate([grad_spread, tail_spread], axis=0)
    byte_act_grad = (byte_grads.astype(f32) + jnp.take(grad_table, slot_idx, axis=0)).astype(bf16)

    grad_scale = 1.0 / math.sqrt(SEQ * BAL)
    grads = jnp.stack([grad_in, grad_out]).reshape(2, NC, 32, hidden) * grad_scale
    mine = lax.dynamic_index_in_dim(grads, core, 1, keepdims=False)
    theirs = lax.dynamic_index_in_dim(grads, 1 - core, 1, keepdims=False)
    final = by_core(core, mine, swap_cores(theirs), 2)
    return (byte_act_grad, final[0], final[1])


def solution(mesh):
    in_specs = (P("seq", "mp"), P("seq", "mp"), P("seq"), P("seq", "mp"), P("seq", "mp"))
    out_specs = (P("seq", "mp"), P("seq", "mp"), P("seq", "mp"))
    return jax.shard_map(local, mesh=mesh, in_specs=in_specs, out_specs=out_specs, check_vma=False)
```

```python
import math

import jax
import jax.numpy as jnp
from jax import lax
from jax.sharding import PartitionSpec as P

BAL = 128
CAP = 224
NY, NZ, NC, NX = 4, 8, 2, 4
SEQ = NY * NZ * NC
epsilon = 1e-05
bf16 = jnp.bfloat16
f32 = jnp.float32


def seq_of(y, z, c):
    return ((y % NY) * NZ + (z % NZ)) * NC + c


def coords_of(s):
    return s // (NZ * NC), (s // NC) % NZ, s % NC


CORE_SWAP = [(s, s ^ 1) for s in range(SEQ)]
ZC_GROUPS = [[seq_of(y, z, c) for z in range(NZ) for c in range(NC)] for y in range(NY)]
YC_GROUPS = [[seq_of(y, z, c) for y in range(NY) for c in range(NC)] for z in range(NZ)]


def y_pairs(step):
    pairs = []
    for s in range(SEQ):
        y, z, c = coords_of(s)
        pairs.append((s, seq_of(y + step, z, c)))
    return pairs


def swap_cores(value):
    return lax.ppermute(value, "seq", CORE_SWAP)


def send_y(value, step):
    return lax.ppermute(value, "seq", y_pairs(step))


def send_x(value, step):
    return lax.ppermute(value, "mp", [(i, (i + step) % NX) for i in range(NX)])


def send_z(value, step):
    pairs = []
    for s in range(SEQ):
        y, z, c = coords_of(s)
        pairs.append((s, seq_of(y, z + step, c)))
    return lax.ppermute(value, "seq", pairs)


def exchange(value, groups):
    return lax.all_to_all(value, "seq", 0, 0, axis_index_groups=groups, tiled=True)


def pick(value, index):
    return lax.dynamic_index_in_dim(value, index, 0, keepdims=False)


def gelu_tanh(values):
    return jax.nn.gelu(values, approximate=True)


def gather_by_y(column, y_idx):
    full = jnp.zeros((NY,) + column.shape, column.dtype)
    full = lax.dynamic_update_index_in_dim(full, column, y_idx, 0)
    for step in (1, 3, 2):
        full = lax.dynamic_update_index_in_dim(
            full, send_y(column, step), (y_idx - step) % NY, 0
        )
    return full


def gather_by_z(block, z_idx):
    full = jnp.zeros((NY, NZ) + block.shape[1:], block.dtype)

    def put(full, value, z, at=0):
        return lax.dynamic_update_slice(full, value[:, None], (at, z % NZ, 0, 0))

    full = put(full, block, z_idx)
    up = down = block
    for hop in (1, 2, 3):
        up, down = send_z(up, 1), send_z(down, -1)
        full = put(put(full, up, z_idx - hop), down, z_idx + hop)
    half = NY // 2
    up, down = send_z(up[:half], 1), send_z(down[half:], -1)
    return put(put(full, up, z_idx + 4), down, z_idx + 4, half)


def reduce_by_y(pieces, y_idx):
    total = pick(pieces, y_idx).astype(f32)
    for step in (1, 3, 2):
        got = send_y(pick(pieces, (y_idx + step) % NY).astype(bf16), step)
        total = total + got.astype(f32)
    return total


def reduce_by_z(pieces, z_idx):
    half = pieces.shape[1] // 2
    far = pick(pieces, (z_idx + 4) % NZ)
    up, down = send_z(far[:half], 1).astype(f32), send_z(far[half:], -1).astype(f32)
    for hop in (3, 2, 1):
        to_up = pick(pieces, (z_idx + hop) % NZ).astype(f32)
        to_down = pick(pieces, (z_idx - hop) % NZ).astype(f32)
        if hop == 3:
            to_up = jnp.concatenate([to_up[:half] + up, to_up[half:]], axis=0)
            to_down = jnp.concatenate([to_down[:half], to_down[half:] + down], axis=0)
        else:
            to_up, to_down = to_up + up, to_down + down
        up = send_z(to_up.astype(bf16), 1).astype(f32)
        down = send_z(to_down.astype(bf16), -1).astype(f32)
    return pick(pieces, z_idx).astype(f32) + up + down


def local(byte_acts, byte_grads, row_of_byte, w_in, w_out):
    quarter = byte_acts.shape[1]
    width = quarter * NX
    hidden = w_in.shape[1] // NC
    shard_idx = lax.axis_index("seq")
    x_idx = lax.axis_index("mp")
    core, z_idx, y_idx = shard_idx % NC, (shard_idx // NC) % NZ, shard_idx // (NZ * NC)

    out_halves = w_out.reshape(1, 32, NC, hidden).swapaxes(1, 2)
    out_copies = jnp.broadcast_to(out_halves, (NY, NC, 32, hidden)).reshape(NY * NC, 32, hidden)
    out_block = exchange(out_copies, YC_GROUPS).reshape(NY, NC * 32, hidden)
    in_halves = w_in.reshape(1, 32, NC, hidden).swapaxes(1, 2)
    in_copies = jnp.broadcast_to(in_halves, (NZ, NC, 32, hidden)).reshape(NZ * NC, 32, hidden)
    in_column = exchange(in_copies, ZC_GROUPS).reshape(NZ * NC * 32, hidden)
    full_w_out = gather_by_z(out_block, z_idx).reshape(width, hidden)
    full_w_in = gather_by_y(in_column, y_idx).reshape(width, hidden)

    local_row = row_of_byte - shard_idx * CAP
    leading = local_row < 0
    slot_idx = jnp.where(leading, CAP, local_row)
    one_hot = (jnp.arange(CAP + 1, dtype=jnp.int32)[:, None] == slot_idx[None, :]).astype(bf16)
    act_sums = jnp.dot(one_hot, byte_acts, preferred_element_type=f32)
    grad_sums = jnp.dot(one_hot, byte_grads, preferred_element_type=f32)
    byte_counts = jnp.sum(one_hot.astype(f32), axis=1)
    own_count = jnp.max(jnp.where(leading, -1, local_row)) + 1
    frag = jnp.stack(
        [act_sums[CAP], grad_sums[CAP], jnp.broadcast_to(byte_counts[CAP], (quarter,))]
    )
    frag = lax.ppermute(frag, "seq", [(s, s - 1) for s in range(1, SEQ)])
    last_mark = (jnp.arange(CAP, dtype=jnp.int32) == own_count - 1).astype(f32)
    act_total = act_sums[:CAP] + last_mark[:, None] * frag[0][None, :]
    grad_total = grad_sums[:CAP] + last_mark[:, None] * frag[1][None, :]
    row_lengths = byte_counts[:CAP] + last_mark * frag[2, 0]
    inv_length = 1.0 / jnp.maximum(row_lengths, 1.0)
    pooled = (act_total * inv_length[:, None]).astype(bf16)
    up_grad = grad_total.astype(bf16)

    rows = jnp.stack([pooled, up_grad])
    wide = jnp.zeros((2, CAP, width), bf16)
    wide = lax.dynamic_update_slice_in_dim(wide, rows, x_idx * quarter, 2)
    for step in (1, 3, 2):
        wide = lax.dynamic_update_slice_in_dim(
            wide, send_x(rows, step), ((x_idx - step) % NX) * quarter, 2
        )
    wide = jnp.concatenate([wide, swap_cores(wide)], axis=1)
    wide_pooled, wide_up = wide[0], wide[1]

    wide_f32 = wide_pooled.astype(f32)
    inv_rms = lax.rsqrt(jnp.mean(wide_f32 * wide_f32, axis=1) + epsilon)
    normed = (wide_f32 * inv_rms[:, None]).astype(bf16)
    pre_act = jnp.dot(normed, full_w_in, preferred_element_type=f32)
    activation = gelu_tanh(pre_act).astype(bf16)
    out_part = lax.dot_general(
        wide_up, activation, (((0,), (0,)), ((), ())), preferred_element_type=f32
    )
    out_rows = reduce_by_z(
        out_part.astype(bf16).reshape(NY, NZ, NC * 32, hidden).swapaxes(0, 1).reshape(
            NZ, NY * NC * 32, hidden
        ),
        z_idx,
    )
    out_rows = exchange(out_rows.astype(bf16).reshape(NY * NC, 32, hidden), YC_GROUPS)
    grad_out = jnp.sum(out_rows.astype(f32).reshape(NY, NC, 32, hidden), axis=0)

    up_proj = jnp.dot(wide_up, full_w_out, preferred_element_type=f32)
    act_grad = jax.vjp(gelu_tanh, pre_act)[1](up_proj)[0].astype(bf16)
    in_part = lax.dot_general(
        normed, act_grad, (((0,), (0,)), ((), ())), preferred_element_type=f32
    )
    in_rows = reduce_by_y(in_part.reshape(NY, NZ * NC * 32, hidden), y_idx)
    in_rows = exchange(in_rows.astype(bf16).reshape(NZ * NC, 32, hidden), ZC_GROUPS)
    grad_in = jnp.sum(in_rows.astype(f32).reshape(NZ, NC, 32, hidden), axis=0)

    normed_part = lax.dot_general(
        act_grad, full_w_in, (((1,), (1,)), ((), ())), preferred_element_type=f32
    )
    stat_part = jnp.sum(act_grad.astype(f32) * pre_act, axis=1) / inv_rms
    stat_high = stat_part.astype(bf16)
    stat_low = (stat_part - stat_high.astype(f32)).astype(bf16)
    lane = jnp.arange(128)[None, :]
    stat_cols = jnp.where(lane == 0, stat_high[:, None], stat_low[:, None])
    stat_cols = jnp.where(lane < 2, stat_cols, jnp.zeros((), bf16))
    sent = jnp.concatenate([normed_part[CAP:].astype(bf16), stat_cols[CAP:]], axis=1)
    got = swap_cores(sent).astype(f32)
    chip_part = normed_part[:CAP] + got[:, :width]
    chip_stat = stat_part[:CAP] + got[:, width] + got[:, width + 1]
    stat_high = chip_stat.astype(bf16)
    stat_low = (chip_stat - stat_high.astype(f32)).astype(bf16)
    stat_cols = jnp.where(lane == 0, stat_high[:, None], stat_low[:, None])
    stat_cols = jnp.where(lane < 2, stat_cols, jnp.zeros((), bf16))
    normed_grad = lax.dynamic_slice_in_dim(chip_part, x_idx * quarter, quarter, 1)
    row_stat = chip_stat
    for step in (1, 3, 2):
        piece = lax.dynamic_slice_in_dim(
            chip_part, ((x_idx + step) % NX) * quarter, quarter, 1
        ).astype(bf16)
        got = send_x(jnp.concatenate([piece, stat_cols], axis=1), step).astype(f32)
        normed_grad = normed_grad + got[:, :quarter]
        row_stat = row_stat + got[:, quarter] + got[:, quarter + 1]
    row_stat = row_stat / width
    own_rms = inv_rms[:CAP]
    pooled_grad = (
        up_grad.astype(f32)
        + own_rms[:, None] * normed_grad
        - pooled.astype(f32) * (own_rms**3 * row_stat)[:, None]
    ).astype(bf16)

    grad_spread = pooled_grad.astype(f32) * inv_length[:, None]
    last_spread = lax.dynamic_slice_in_dim(grad_spread, own_count - 1, 1, 0)
    tail_spread = lax.ppermute(last_spread, "seq", [(s, s + 1) for s in range(SEQ - 1)])
    grad_table = jnp.concatenate([grad_spread, tail_spread], axis=0)
    byte_act_grad = (byte_grads.astype(f32) + jnp.take(grad_table, slot_idx, axis=0)).astype(bf16)

    grad_scale = 1.0 / math.sqrt(SEQ * BAL)
    grad_in = grad_in.swapaxes(0, 1).reshape(32, NC * hidden) * grad_scale
    grad_out = grad_out.swapaxes(0, 1).reshape(32, NC * hidden) * grad_scale
    return (byte_act_grad, grad_in, grad_out)


def solution(mesh):
    in_specs = (P("seq", "mp"), P("seq", "mp"), P("seq"), P("seq", "mp"), P("seq", "mp"))
    out_specs = (P("seq", "mp"), P("seq", "mp"), P("seq", "mp"))
    return jax.shard_map(local, mesh=mesh, in_specs=in_specs, out_specs=out_specs, check_vma=False)
```

```python
import math

import jax
import jax.numpy as jnp
from jax import lax
from jax.experimental import pallas as pl
from jax.experimental.pallas import tpu as pltpu
from jax.sharding import PartitionSpec as P

BAL = 128
CAP = 224
NY, NZ, NC, NX = 4, 8, 2, 4
SEQ = NY * NZ * NC
epsilon = 1e-05
bf16 = jnp.bfloat16
f32 = jnp.float32


def seq_of(y, z, c):
    return ((y % NY) * NZ + (z % NZ)) * NC + c


def coords_of(s):
    return s // (NZ * NC), (s // NC) % NZ, s % NC


CORE_SWAP = [(s, s ^ 1) for s in range(SEQ)]
ZC_GROUPS = [[seq_of(y, z, c) for z in range(NZ) for c in range(NC)] for y in range(NY)]
YC_GROUPS = [[seq_of(y, z, c) for y in range(NY) for c in range(NC)] for z in range(NZ)]


def y_pairs(step):
    pairs = []
    for s in range(SEQ):
        y, z, c = coords_of(s)
        pairs.append((s, seq_of(y + step, z, c)))
    return pairs


def swap_cores(value):
    return lax.ppermute(value, "seq", CORE_SWAP)


def send_y(value, step):
    return lax.ppermute(value, "seq", y_pairs(step))


def send_x(value, step):
    return lax.ppermute(value, "mp", [(i, (i + step) % NX) for i in range(NX)])


def send_z(value, step):
    pairs = []
    for s in range(SEQ):
        y, z, c = coords_of(s)
        pairs.append((s, seq_of(y, z + step, c)))
    return lax.ppermute(value, "seq", pairs)


def exchange(value, groups):
    return lax.all_to_all(value, "seq", 0, 0, axis_index_groups=groups, tiled=True)


def pick(value, index):
    return lax.dynamic_index_in_dim(value, index, 0, keepdims=False)


def gelu_tanh(values):
    return jax.nn.gelu(values, approximate=True)


def by_core(core, own, other, axis):
    first = jnp.where(core == 0, own, other)
    second = jnp.where(core == 0, other, own)
    return jnp.concatenate([first, second], axis=axis)


def by_y(parts, y_idx):
    own, before, after, far = parts
    order = []
    for y in range(NY):
        step = (y_idx - y) % NY
        order.append(
            jnp.where(
                step == 0,
                own,
                jnp.where(step == 1, before, jnp.where(step == 3, after, far)),
            )
        )
    return jnp.stack(order)


def gather_by_y(column):
    return [column] + [send_y(column, step) for step in (1, 3, 2)]


def gather_by_z(block):
    pieces = [block]
    up = down = block
    for hop in (1, 2, 3):
        up, down = send_z(up, 1), send_z(down, -1)
        pieces += [up, down]
    half = NY // 2
    return pieces + [send_z(up[:half], 1), send_z(down[half:], -1)]


def assemble_kernel(at_ref, *refs):
    in_parts, out_parts, row_parts = refs[:4], refs[4:13], refs[13:21]
    w_in_ref, w_out_ref, pooled_ref, up_ref, sems = refs[21:]
    x_idx, y_idx, z_idx = at_ref[0], at_ref[1], at_ref[2]
    copies = []

    def copy(source, target):
        copies.append(pltpu.make_async_copy(source, target, sems.at[len(copies)]))

    steps = (0, 1, 3, 2)
    depth = in_parts[0].shape[0]
    for part, step in zip(in_parts, steps):
        copy(part, w_in_ref.at[lax.rem(y_idx + NY - step, NY)])
    deep = out_parts[0].shape[1]
    for n, part in enumerate(out_parts):
        hop = (n + 1) // 2
        z = lax.rem(z_idx + NZ + (hop if n % 2 == 0 else -hop), NZ)
        ys = pl.ds(0 if n != 8 else NY // 2, part.shape[0])
        copy(part, w_out_ref.at[ys, pl.ds(pl.multiple_of(z * deep, deep), deep)])
    rows, quarter = row_parts[0].shape[1:]
    for n, part in enumerate(row_parts):
        x = lax.rem(x_idx + NX - steps[n % 4], NX)
        where = (
            pl.ds((n // 4) * rows, rows),
            pl.ds(pl.multiple_of(x * quarter, quarter), quarter),
        )
        copy(part.at[0], pooled_ref.at[where])
        copy(part.at[1], up_ref.at[where])
    for item in copies:
        item.start()
    for item in copies:
        item.wait()


def assemble(at, in_parts, out_parts, row_parts):
    depth, hidden = in_parts[0].shape
    rows, quarter = row_parts[0].shape[1:]
    weight = jax.ShapeDtypeStruct((NY, depth, hidden), bf16)
    wide = jax.ShapeDtypeStruct((2 * rows, NX * quarter), bf16)
    moved = 2 * (2 * NY * depth * hidden + 4 * rows * NX * quarter)
    return pl.pallas_call(
        assemble_kernel,
        out_shape=(weight, weight, wide, wide),
        in_specs=[pl.BlockSpec(memory_space=pltpu.SMEM)]
        + [pl.BlockSpec(memory_space=pl.ANY)] * 21,
        out_specs=(pl.BlockSpec(memory_space=pltpu.VMEM),) * 4,
        scratch_shapes=[pltpu.SemaphoreType.DMA((29,))],
        cost_estimate=pl.CostEstimate(flops=0, bytes_accessed=2 * moved, transcendentals=0),
        name="assemble",
    )(at, *in_parts, *out_parts, *row_parts)


def reduce_by_y(pieces, y_idx):
    total = pick(pieces, y_idx).astype(f32)
    for step in (1, 3, 2):
        got = send_y(pick(pieces, (y_idx + step) % NY).astype(bf16), step)
        total = total + got.astype(f32)
    return total


def reduce_by_z(pieces, z_idx):
    half = pieces.shape[1] // 2
    far = pick(pieces, (z_idx + 4) % NZ)
    up, down = send_z(far[:half], 1).astype(f32), send_z(far[half:], -1).astype(f32)
    for hop in (3, 2, 1):
        to_up = pick(pieces, (z_idx + hop) % NZ).astype(f32)
        to_down = pick(pieces, (z_idx - hop) % NZ).astype(f32)
        if hop == 3:
            to_up = jnp.concatenate([to_up[:half] + up, to_up[half:]], axis=0)
            to_down = jnp.concatenate([to_down[:half], to_down[half:] + down], axis=0)
        else:
            to_up, to_down = to_up + up, to_down + down
        up = send_z(to_up.astype(bf16), 1).astype(f32)
        down = send_z(to_down.astype(bf16), -1).astype(f32)
    return pick(pieces, z_idx).astype(f32) + up + down


def local(byte_acts, byte_grads, row_of_byte, w_in, w_out):
    quarter = byte_acts.shape[1]
    width = quarter * NX
    hidden = w_in.shape[1] // NC
    shard_idx = lax.axis_index("seq")
    x_idx = lax.axis_index("mp")
    core, z_idx, y_idx = shard_idx % NC, (shard_idx // NC) % NZ, shard_idx // (NZ * NC)

    in_halves = w_in.reshape(1, 32, NC, hidden).swapaxes(1, 2)
    in_copies = jnp.broadcast_to(in_halves, (NZ, NC, 32, hidden)).reshape(NZ * NC, 32, hidden)
    in_column = exchange(in_copies, ZC_GROUPS).reshape(NZ * NC * 32, hidden)
    out_halves = w_out.reshape(32, NC, hidden)
    keep = lax.dynamic_index_in_dim(out_halves, core, 1, keepdims=False)
    give = lax.dynamic_index_in_dim(out_halves, 1 - core, 1, keepdims=False)
    out_rows = by_core(core, keep, swap_cores(give), 0)
    out_block = by_y(gather_by_y(out_rows), y_idx)
    out_parts = gather_by_z(out_block)
    in_parts = gather_by_y(in_column)

    local_row = row_of_byte - shard_idx * CAP
    leading = local_row < 0
    slot_idx = jnp.where(leading, CAP, local_row)
    one_hot = (jnp.arange(CAP + 1, dtype=jnp.int32)[:, None] == slot_idx[None, :]).astype(bf16)
    act_sums = jnp.dot(one_hot, byte_acts, preferred_element_type=f32)
    grad_sums = jnp.dot(one_hot, byte_grads, preferred_element_type=f32)
    byte_counts = jnp.sum(one_hot.astype(f32), axis=1)
    own_count = jnp.max(jnp.where(leading, -1, local_row)) + 1
    frag = jnp.stack(
        [act_sums[CAP], grad_sums[CAP], jnp.broadcast_to(byte_counts[CAP], (quarter,))]
    )
    frag = lax.ppermute(frag, "seq", [(s, s - 1) for s in range(1, SEQ)])
    last_mark = (jnp.arange(CAP, dtype=jnp.int32) == own_count - 1).astype(f32)
    act_total = act_sums[:CAP] + last_mark[:, None] * frag[0][None, :]
    grad_total = grad_sums[:CAP] + last_mark[:, None] * frag[1][None, :]
    row_lengths = byte_counts[:CAP] + last_mark * frag[2, 0]
    inv_length = 1.0 / jnp.maximum(row_lengths, 1.0)
    pooled = (act_total * inv_length[:, None]).astype(bf16)
    up_grad = grad_total.astype(bf16)

    rows = jnp.stack([pooled, up_grad])
    own_parts = [rows] + [send_x(rows, step) for step in (1, 3, 2)]
    row_parts = own_parts + [swap_cores(part) for part in own_parts]
    at = jnp.stack([x_idx, y_idx, z_idx]).astype(jnp.int32)
    full_w_in, full_w_out, wide_pooled, wide_up = assemble(at, in_parts, out_parts, row_parts)
    full_w_in = full_w_in.reshape(width, hidden)
    full_w_out = full_w_out.reshape(width, hidden)

    wide_f32 = wide_pooled.astype(f32)
    inv_rms = lax.rsqrt(jnp.mean(wide_f32 * wide_f32, axis=1) + epsilon)
    normed = (wide_f32 * inv_rms[:, None]).astype(bf16)
    pre_act = jnp.dot(normed, full_w_in, preferred_element_type=f32)
    activation = gelu_tanh(pre_act).astype(bf16)
    out_part = lax.dot_general(
        wide_up, activation, (((0,), (0,)), ((), ())), preferred_element_type=f32
    )
    out_rows = reduce_by_z(
        out_part.astype(bf16).reshape(NY, NZ, NC * 32, hidden).swapaxes(0, 1).reshape(
            NZ, NY * NC * 32, hidden
        ),
        z_idx,
    )
    out_rows = exchange(out_rows.astype(bf16).reshape(NY * NC, 32, hidden), YC_GROUPS)
    grad_out = jnp.sum(out_rows.astype(f32).reshape(NY, NC, 32, hidden), axis=0)

    up_proj = jnp.dot(wide_up, full_w_out, preferred_element_type=f32)
    act_grad = jax.vjp(gelu_tanh, pre_act)[1](up_proj)[0].astype(bf16)
    in_part = lax.dot_general(
        normed, act_grad, (((0,), (0,)), ((), ())), preferred_element_type=f32
    )
    in_rows = reduce_by_y(in_part.reshape(NY, NZ * NC * 32, hidden), y_idx)
    in_rows = exchange(in_rows.astype(bf16).reshape(NZ * NC, 32, hidden), ZC_GROUPS)
    grad_in = jnp.sum(in_rows.astype(f32).reshape(NZ, NC, 32, hidden), axis=0)

    normed_part = lax.dot_general(
        act_grad, full_w_in, (((1,), (1,)), ((), ())), preferred_element_type=f32
    )
    stat_part = jnp.sum(act_grad.astype(f32) * pre_act, axis=1) / inv_rms
    stat_high = stat_part.astype(bf16)
    stat_low = (stat_part - stat_high.astype(f32)).astype(bf16)
    lane = jnp.arange(128)[None, :]
    stat_cols = jnp.where(lane == 0, stat_high[:, None], stat_low[:, None])
    stat_cols = jnp.where(lane < 2, stat_cols, jnp.zeros((), bf16))
    sent = jnp.concatenate([normed_part[CAP:].astype(bf16), stat_cols[CAP:]], axis=1)
    got = swap_cores(sent).astype(f32)
    chip_part = normed_part[:CAP] + got[:, :width]
    chip_stat = stat_part[:CAP] + got[:, width] + got[:, width + 1]
    stat_high = chip_stat.astype(bf16)
    stat_low = (chip_stat - stat_high.astype(f32)).astype(bf16)
    stat_cols = jnp.where(lane == 0, stat_high[:, None], stat_low[:, None])
    stat_cols = jnp.where(lane < 2, stat_cols, jnp.zeros((), bf16))
    normed_grad = lax.dynamic_slice_in_dim(chip_part, x_idx * quarter, quarter, 1)
    row_stat = chip_stat
    for step in (1, 3, 2):
        piece = lax.dynamic_slice_in_dim(
            chip_part, ((x_idx + step) % NX) * quarter, quarter, 1
        ).astype(bf16)
        got = send_x(jnp.concatenate([piece, stat_cols], axis=1), step).astype(f32)
        normed_grad = normed_grad + got[:, :quarter]
        row_stat = row_stat + got[:, quarter] + got[:, quarter + 1]
    row_stat = row_stat / width
    own_rms = inv_rms[:CAP]
    pooled_grad = (
        up_grad.astype(f32)
        + own_rms[:, None] * normed_grad
        - pooled.astype(f32) * (own_rms**3 * row_stat)[:, None]
    ).astype(bf16)

    grad_spread = pooled_grad.astype(f32) * inv_length[:, None]
    last_spread = lax.dynamic_slice_in_dim(grad_spread, own_count - 1, 1, 0)
    tail_spread = lax.ppermute(last_spread, "seq", [(s, s + 1) for s in range(SEQ - 1)])
    grad_table = jnp.concatenate([grad_spread, tail_spread], axis=0)
    byte_act_grad = (byte_grads.astype(f32) + jnp.take(grad_table, slot_idx, axis=0)).astype(bf16)

    grad_scale = 1.0 / math.sqrt(SEQ * BAL)
    grad_in = grad_in.swapaxes(0, 1).reshape(32, NC * hidden) * grad_scale
    grad_out = grad_out.swapaxes(0, 1).reshape(32, NC * hidden) * grad_scale
    return (byte_act_grad, grad_in, grad_out)


def solution(mesh):
    in_specs = (P("seq", "mp"), P("seq", "mp"), P("seq"), P("seq", "mp"), P("seq", "mp"))
    out_specs = (P("seq", "mp"), P("seq", "mp"), P("seq", "mp"))
    return jax.shard_map(local, mesh=mesh, in_specs=in_specs, out_specs=out_specs, check_vma=False)
```

```python
import math

import jax
import jax.numpy as jnp
from jax import lax
from jax.experimental import pallas as pl
from jax.experimental.pallas import tpu as pltpu
from jax.sharding import PartitionSpec as P

BAL = 128
CAP = 224
NY, NZ, NC, NX = 4, 8, 2, 4
SEQ = NY * NZ * NC
epsilon = 1e-05
bf16 = jnp.bfloat16
f32 = jnp.float32


def seq_of(y, z, c):
    return ((y % NY) * NZ + (z % NZ)) * NC + c


def coords_of(s):
    return s // (NZ * NC), (s // NC) % NZ, s % NC


CORE_SWAP = [(s, s ^ 1) for s in range(SEQ)]
ZC_GROUPS = [[seq_of(y, z, c) for z in range(NZ) for c in range(NC)] for y in range(NY)]


def y_pairs(step):
    pairs = []
    for s in range(SEQ):
        y, z, c = coords_of(s)
        pairs.append((s, seq_of(y + step, z, c)))
    return pairs


def swap_cores(value):
    return lax.ppermute(value, "seq", CORE_SWAP)


def send_y(value, step):
    return lax.ppermute(value, "seq", y_pairs(step))


def send_x(value, step):
    return lax.ppermute(value, "mp", [(i, (i + step) % NX) for i in range(NX)])


def send_z(value, step):
    pairs = []
    for s in range(SEQ):
        y, z, c = coords_of(s)
        pairs.append((s, seq_of(y, z + step, c)))
    return lax.ppermute(value, "seq", pairs)


def exchange(value, groups):
    return lax.all_to_all(value, "seq", 0, 0, axis_index_groups=groups, tiled=True)


def pick(value, index):
    return lax.dynamic_index_in_dim(value, index, 0, keepdims=False)


def gelu_tanh(values):
    return jax.nn.gelu(values, approximate=True)


def by_core(core, own, other, axis):
    first = jnp.where(core == 0, own, other)
    second = jnp.where(core == 0, other, own)
    return jnp.concatenate([first, second], axis=axis)


def by_y(parts, y_idx):
    own, before, after, far = parts
    order = []
    for y in range(NY):
        step = (y_idx - y) % NY
        order.append(
            jnp.where(
                step == 0,
                own,
                jnp.where(step == 1, before, jnp.where(step == 3, after, far)),
            )
        )
    return jnp.stack(order)


def gather_by_y(column):
    return [column] + [send_y(column, step) for step in (1, 3, 2)]


def gather_by_z(block):
    pieces = [block]
    up = down = block
    for _ in range(3):
        up, down = send_z(up, 1), send_z(down, -1)
        pieces += [up, down]
    half = NY // 2
    return pieces + [send_z(up[:half], 1), send_z(down[half:], -1)]


def assemble_kernel(at_ref, *refs):
    in_parts, out_parts, row_parts = refs[:4], refs[4:13], refs[13:15]
    w_in_ref, w_out_ref, pooled_ref, up_ref, sems = refs[15:]
    x_idx, y_idx, z_idx = at_ref[0], at_ref[1], at_ref[2]
    copies = []

    def copy(source, target):
        copies.append(pltpu.make_async_copy(source, target, sems.at[len(copies)]))

    steps = (0, 1, 3, 2)
    for part, step in zip(in_parts, steps):
        copy(part, w_in_ref.at[lax.rem(y_idx + NY - step, NY)])
    deep = out_parts[0].shape[1]
    for n, part in enumerate(out_parts):
        hop = (n + 1) // 2
        z = lax.rem(z_idx + NZ + (hop if n % 2 == 0 else -hop), NZ)
        ys = pl.ds(0 if n != 8 else NY // 2, part.shape[0])
        copy(part, w_out_ref.at[ys, pl.ds(pl.multiple_of(z * deep, deep), deep)])
    rows, quarter = row_parts[0].shape[2:]
    for half, part in enumerate(row_parts):
        for n, step in enumerate(steps):
            x = lax.rem(x_idx + NX - step, NX)
            where = (
                pl.ds(half * rows, rows),
                pl.ds(pl.multiple_of(x * quarter, quarter), quarter),
            )
            copy(part.at[n, 0], pooled_ref.at[where])
            copy(part.at[n, 1], up_ref.at[where])
    for item in copies:
        item.start()
    for item in copies:
        item.wait()


def assemble(at, in_parts, out_parts, row_parts):
    depth, hidden = in_parts[0].shape
    rows, quarter = row_parts[0].shape[2:]
    weight = jax.ShapeDtypeStruct((NY, depth, hidden), bf16)
    wide = jax.ShapeDtypeStruct((2 * rows, NX * quarter), bf16)
    moved = 2 * (2 * NY * depth * hidden + 4 * rows * NX * quarter)
    return pl.pallas_call(
        assemble_kernel,
        out_shape=(weight, weight, wide, wide),
        in_specs=[pl.BlockSpec(memory_space=pltpu.SMEM)]
        + [pl.BlockSpec(memory_space=pl.ANY)] * 15,
        out_specs=(pl.BlockSpec(memory_space=pltpu.VMEM),) * 4,
        scratch_shapes=[pltpu.SemaphoreType.DMA((29,))],
        cost_estimate=pl.CostEstimate(flops=0, bytes_accessed=2 * moved, transcendentals=0),
        name="assemble",
    )(at, *in_parts, *out_parts, *row_parts)


def reduce_by_y(pieces, y_idx):
    total = pick(pieces, y_idx).astype(f32)
    for step in (1, 3, 2):
        got = send_y(pick(pieces, (y_idx + step) % NY).astype(bf16), step)
        total = total + got.astype(f32)
    return total


def reduce_by_z(pieces, z_idx):
    half = pieces.shape[1] // 2
    far = pick(pieces, (z_idx + 4) % NZ)
    up, down = send_z(far[:half], 1).astype(f32), send_z(far[half:], -1).astype(f32)
    for hop in (3, 2, 1):
        to_up = pick(pieces, (z_idx + hop) % NZ).astype(f32)
        to_down = pick(pieces, (z_idx - hop) % NZ).astype(f32)
        if hop == 3:
            to_up = jnp.concatenate([to_up[:half] + up, to_up[half:]], axis=0)
            to_down = jnp.concatenate([to_down[:half], to_down[half:] + down], axis=0)
        else:
            to_up, to_down = to_up + up, to_down + down
        up = send_z(to_up.astype(bf16), 1).astype(f32)
        down = send_z(to_down.astype(bf16), -1).astype(f32)
    return pick(pieces, z_idx).astype(f32) + up + down


def local(byte_acts, byte_grads, row_of_byte, w_in, w_out):
    quarter = byte_acts.shape[1]
    width = quarter * NX
    hidden = w_in.shape[1] // NC
    shard_idx = lax.axis_index("seq")
    x_idx = lax.axis_index("mp")
    core, z_idx, y_idx = shard_idx % NC, (shard_idx // NC) % NZ, shard_idx // (NZ * NC)

    in_halves = w_in.reshape(1, 32, NC, hidden).swapaxes(1, 2)
    in_copies = jnp.broadcast_to(in_halves, (NZ, NC, 32, hidden)).reshape(NZ * NC, 32, hidden)
    in_column = exchange(in_copies, ZC_GROUPS).reshape(NZ * NC * 32, hidden)
    out_halves = w_out.reshape(32, NC, hidden)
    keep = lax.dynamic_index_in_dim(out_halves, core, 1, keepdims=False)
    give = lax.dynamic_index_in_dim(out_halves, 1 - core, 1, keepdims=False)
    out_rows = by_core(core, keep, swap_cores(give), 0)
    out_block = by_y(gather_by_y(out_rows), y_idx)
    out_parts = gather_by_z(out_block)
    in_parts = gather_by_y(in_column)

    local_row = row_of_byte - shard_idx * CAP
    leading = local_row < 0
    slot_idx = jnp.where(leading, CAP, local_row)
    one_hot = (jnp.arange(CAP + 1, dtype=jnp.int32)[:, None] == slot_idx[None, :]).astype(bf16)
    act_sums = jnp.dot(one_hot, byte_acts, preferred_element_type=f32)
    grad_sums = jnp.dot(one_hot, byte_grads, preferred_element_type=f32)
    byte_counts = jnp.sum(one_hot.astype(f32), axis=1)
    own_count = jnp.max(jnp.where(leading, -1, local_row)) + 1
    frag = jnp.stack(
        [act_sums[CAP], grad_sums[CAP], jnp.broadcast_to(byte_counts[CAP], (quarter,))]
    )
    frag = lax.ppermute(frag, "seq", [(s, s - 1) for s in range(1, SEQ)])
    last_mark = (jnp.arange(CAP, dtype=jnp.int32) == own_count - 1).astype(f32)
    act_total = act_sums[:CAP] + last_mark[:, None] * frag[0][None, :]
    grad_total = grad_sums[:CAP] + last_mark[:, None] * frag[1][None, :]
    row_lengths = byte_counts[:CAP] + last_mark * frag[2, 0]
    inv_length = 1.0 / jnp.maximum(row_lengths, 1.0)
    pooled = (act_total * inv_length[:, None]).astype(bf16)
    up_grad = grad_total.astype(bf16)

    rows = jnp.stack([pooled, up_grad])
    own_parts = jnp.stack([rows] + [send_x(rows, step) for step in (1, 3, 2)])
    row_parts = [own_parts, swap_cores(own_parts)]
    at = jnp.stack([x_idx, y_idx, z_idx]).astype(jnp.int32)
    full_w_in, full_w_out, wide_pooled, wide_up = assemble(at, in_parts, out_parts, row_parts)
    full_w_in = full_w_in.reshape(width, hidden)
    full_w_out = full_w_out.reshape(width, hidden)

    wide_f32 = wide_pooled.astype(f32)
    inv_rms = lax.rsqrt(jnp.mean(wide_f32 * wide_f32, axis=1) + epsilon)
    normed = (wide_f32 * inv_rms[:, None]).astype(bf16)
    pre_act = jnp.dot(normed, full_w_in, preferred_element_type=f32)
    activation = gelu_tanh(pre_act).astype(bf16)
    out_part = lax.dot_general(
        wide_up, activation, (((0,), (0,)), ((), ())), preferred_element_type=f32
    )
    out_rows = reduce_by_z(
        out_part.astype(bf16).reshape(NY, NZ, NC * 32, hidden).swapaxes(0, 1).reshape(
            NZ, NY * NC * 32, hidden
        ),
        z_idx,
    )
    up_proj = jnp.dot(wide_up, full_w_out, preferred_element_type=f32)
    act_grad = jax.vjp(gelu_tanh, pre_act)[1](up_proj)[0].astype(bf16)
    stat_part = jnp.sum(act_grad.astype(f32) * pre_act, axis=1) / inv_rms
    in_part = lax.dot_general(
        normed, act_grad, (((0,), (0,)), ((), ())), preferred_element_type=f32
    ).astype(bf16)
    out_rows = reduce_by_y(out_rows.reshape(NY, NC * 32, hidden), y_idx).reshape(NC, 32, hidden)
    out_mine = pick(out_rows, core)
    out_theirs = swap_cores(pick(out_rows, 1 - core))
    grad_out = by_core(core, out_mine, out_theirs, 1)

    in_rows = reduce_by_y(in_part.reshape(NY, NZ * NC * 32, hidden), y_idx)
    in_rows = exchange(in_rows.astype(bf16).reshape(NZ * NC, 32, hidden), ZC_GROUPS)
    grad_in = jnp.sum(in_rows.astype(f32).reshape(NZ, NC, 32, hidden), axis=0)

    normed_part = lax.dot_general(
        act_grad, full_w_in, (((1,), (1,)), ((), ())), preferred_element_type=f32
    )
    stat_high = stat_part.astype(bf16)
    stat_low = (stat_part - stat_high.astype(f32)).astype(bf16)
    lane = jnp.arange(128)[None, :]
    stat_cols = jnp.where(lane == 0, stat_high[:, None], stat_low[:, None])
    stat_cols = jnp.where(lane < 2, stat_cols, jnp.zeros((), bf16))
    sent = jnp.concatenate([normed_part[CAP:].astype(bf16), stat_cols[CAP:]], axis=1)
    got = swap_cores(sent)
    got = got.astype(f32)
    chip_part = normed_part[:CAP] + got[:, :width]
    chip_stat = stat_part[:CAP] + got[:, width] + got[:, width + 1]
    stat_high = chip_stat.astype(bf16)
    stat_low = (chip_stat - stat_high.astype(f32)).astype(bf16)
    stat_cols = jnp.where(lane == 0, stat_high[:, None], stat_low[:, None])
    stat_cols = jnp.where(lane < 2, stat_cols, jnp.zeros((), bf16))
    normed_grad = lax.dynamic_slice_in_dim(chip_part, x_idx * quarter, quarter, 1)
    row_stat = chip_stat
    for step in (1, 3, 2):
        piece = lax.dynamic_slice_in_dim(
            chip_part, ((x_idx + step) % NX) * quarter, quarter, 1
        ).astype(bf16)
        piece = jnp.concatenate([piece, stat_cols], axis=1)
        got = send_x(piece, step)
        got = got.astype(f32)
        normed_grad = normed_grad + got[:, :quarter]
        row_stat = row_stat + got[:, quarter] + got[:, quarter + 1]
    row_stat = row_stat / width
    own_rms = inv_rms[:CAP]
    pooled_grad = (
        up_grad.astype(f32)
        + own_rms[:, None] * normed_grad
        - pooled.astype(f32) * (own_rms**3 * row_stat)[:, None]
    ).astype(bf16)

    grad_spread = pooled_grad.astype(f32) * inv_length[:, None]
    last_spread = lax.dynamic_slice_in_dim(grad_spread, own_count - 1, 1, 0)
    tail_spread = lax.ppermute(last_spread, "seq", [(s, s + 1) for s in range(SEQ - 1)])
    grad_table = jnp.concatenate([grad_spread, tail_spread], axis=0)
    byte_act_grad = (byte_grads.astype(f32) + jnp.take(grad_table, slot_idx, axis=0)).astype(bf16)

    grad_scale = 1.0 / math.sqrt(SEQ * BAL)
    grad_in = grad_in.swapaxes(0, 1).reshape(32, NC * hidden) * grad_scale
    return (byte_act_grad, grad_in, grad_out * grad_scale)


def solution(mesh):
    in_specs = (P("seq", "mp"), P("seq", "mp"), P("seq"), P("seq", "mp"), P("seq", "mp"))
    out_specs = (P("seq", "mp"), P("seq", "mp"), P("seq", "mp"))

    return jax.shard_map(local, mesh=mesh, in_specs=in_specs, out_specs=out_specs, check_vma=False)
```

```python
import math

import jax
import jax.numpy as jnp
from jax import lax
from jax.experimental import pallas as pl
from jax.experimental.pallas import tpu as pltpu
from jax.sharding import PartitionSpec as P

BAL = 128
CAP = 224
NY, NZ, NC, NX = 4, 8, 2, 4
SEQ = NY * NZ * NC
epsilon = 1e-05
bf16 = jnp.bfloat16
f32 = jnp.float32


def seq_of(y, z, c):
    return ((y % NY) * NZ + (z % NZ)) * NC + c


def coords_of(s):
    return s // (NZ * NC), (s // NC) % NZ, s % NC


CORE_SWAP = [(s, s ^ 1) for s in range(SEQ)]
ZC_GROUPS = [[seq_of(y, z, c) for z in range(NZ) for c in range(NC)] for y in range(NY)]


def y_pairs(step):
    pairs = []
    for s in range(SEQ):
        y, z, c = coords_of(s)
        pairs.append((s, seq_of(y + step, z, c)))
    return pairs


def swap_cores(value):
    return lax.ppermute(value, "seq", CORE_SWAP)


def send_y(value, step):
    return lax.ppermute(value, "seq", y_pairs(step))


def send_x(value, step):
    return lax.ppermute(value, "mp", [(i, (i + step) % NX) for i in range(NX)])


def exchange(value, groups):
    return lax.all_to_all(value, "seq", 0, 0, axis_index_groups=groups, tiled=True)


def pick(value, index):
    return lax.dynamic_index_in_dim(value, index, 0, keepdims=False)


def gelu_tanh(values):
    return jax.nn.gelu(values, approximate=True)


def gather_by_y(column):
    return [column] + [send_y(column, step) for step in (1, 3, 2)]


def start_and_wait(pairs, sems):
    copies = [
        pltpu.make_async_copy(source, target, sems.at[n])
        for n, (source, target) in enumerate(pairs)
    ]
    for item in copies:
        item.start()
    for item in copies:
        item.wait()


STEPS = (0, 1, 3, 2)


def weight_kernel(at_ref, *refs):
    parts, (full_ref, sems) = refs[:4], refs[4:]
    pairs = [
        (part, full_ref.at[lax.rem(at_ref[1] + NY - step, NY)])
        for part, step in zip(parts, STEPS)
    ]
    start_and_wait(pairs, sems)


def rows_kernel(at_ref, own_ref, other_ref, pooled_ref, up_ref, sems):
    rows, quarter = own_ref.shape[2:]
    pairs = []
    for half, part in enumerate((own_ref, other_ref)):
        for n, step in enumerate(STEPS):
            x = lax.rem(at_ref[0] + NX - step, NX)
            where = (
                pl.ds(half * rows, rows),
                pl.ds(pl.multiple_of(x * quarter, quarter), quarter),
            )
            pairs.append((part.at[n, 0], pooled_ref.at[where]))
            pairs.append((part.at[n, 1], up_ref.at[where]))
    start_and_wait(pairs, sems)


def place(kernel, at, parts, shapes, n_copies):
    moved = sum(2 * math.prod(shape) for shape in shapes)
    return pl.pallas_call(
        kernel,
        out_shape=tuple(jax.ShapeDtypeStruct(shape, bf16) for shape in shapes),
        in_specs=[pl.BlockSpec(memory_space=pltpu.SMEM)]
        + [pl.BlockSpec(memory_space=pl.ANY)] * len(parts),
        out_specs=(pl.BlockSpec(memory_space=pltpu.VMEM),) * len(shapes),
        scratch_shapes=[pltpu.SemaphoreType.DMA((n_copies,))],
        cost_estimate=pl.CostEstimate(flops=0, bytes_accessed=2 * moved, transcendentals=0),
    )(at, *parts)


def place_weight(at, parts):
    depth, hidden = parts[0].shape
    (full,) = place(weight_kernel, at, parts, [(NY, depth, hidden)], 4)
    return full.reshape(NY * depth, hidden)


def place_rows(at, own_parts, other_parts):
    rows, quarter = own_parts.shape[2:]
    wide = (2 * rows, NX * quarter)
    return place(rows_kernel, at, [own_parts, other_parts], [wide, wide], 16)


def reduce_by_y(pieces, y_idx):
    total = pick(pieces, y_idx).astype(f32)
    for step in (1, 3, 2):
        got = send_y(pick(pieces, (y_idx + step) % NY).astype(bf16), step)
        total = total + got.astype(f32)
    return total


def local(byte_acts, byte_grads, row_of_byte, w_in, w_out):
    quarter = byte_acts.shape[1]
    width = quarter * NX
    hidden = w_in.shape[1] // NC
    shard_idx = lax.axis_index("seq")
    x_idx = lax.axis_index("mp")
    y_idx = shard_idx // (NZ * NC)

    def spread(weight):
        halves = weight.reshape(1, 32, NC, hidden).swapaxes(1, 2)
        copies = jnp.broadcast_to(halves, (NZ, NC, 32, hidden)).reshape(NZ * NC, 32, hidden)
        return exchange(copies, ZC_GROUPS).reshape(NZ * NC * 32, hidden)

    in_column = spread(w_in)
    in_parts = gather_by_y(in_column)
    out_column = spread(w_out)
    out_parts = gather_by_y(out_column)

    local_row = row_of_byte - shard_idx * CAP
    leading = local_row < 0
    slot_idx = jnp.where(leading, CAP, local_row)
    one_hot = (jnp.arange(CAP + 1, dtype=jnp.int32)[:, None] == slot_idx[None, :]).astype(bf16)
    act_sums = jnp.dot(one_hot, byte_acts, preferred_element_type=f32)
    grad_sums = jnp.dot(one_hot, byte_grads, preferred_element_type=f32)
    byte_counts = jnp.sum(one_hot.astype(f32), axis=1)
    own_count = jnp.max(jnp.where(leading, -1, local_row)) + 1
    frag = jnp.stack(
        [act_sums[CAP], grad_sums[CAP], jnp.broadcast_to(byte_counts[CAP], (quarter,))]
    )
    frag = lax.ppermute(frag, "seq", [(s, s - 1) for s in range(1, SEQ)])
    last_mark = (jnp.arange(CAP, dtype=jnp.int32) == own_count - 1).astype(f32)
    act_total = act_sums[:CAP] + last_mark[:, None] * frag[0][None, :]
    grad_total = grad_sums[:CAP] + last_mark[:, None] * frag[1][None, :]
    row_lengths = byte_counts[:CAP] + last_mark * frag[2, 0]
    inv_length = 1.0 / jnp.maximum(row_lengths, 1.0)
    pooled = (act_total * inv_length[:, None]).astype(bf16)
    up_grad = grad_total.astype(bf16)

    rows = jnp.stack([pooled, up_grad])
    own_parts = [rows] + [send_x(rows, step) for step in (1, 3, 2)]
    own_parts = jnp.stack(own_parts)
    other_parts = swap_cores(own_parts)
    at = jnp.stack([x_idx, y_idx]).astype(jnp.int32)
    wide_pooled, wide_up = place_rows(at, own_parts, other_parts)
    full_w_in = place_weight(at, in_parts)
    full_w_out = place_weight(at, out_parts)

    wide_f32 = wide_pooled.astype(f32)
    inv_rms = lax.rsqrt(jnp.mean(wide_f32 * wide_f32, axis=1) + epsilon)
    normed = (wide_f32 * inv_rms[:, None]).astype(bf16)
    pre_act = jnp.dot(normed, full_w_in, preferred_element_type=f32)
    activation = gelu_tanh(pre_act).astype(bf16)
    out_part = lax.dot_general(
        wide_up, activation, (((0,), (0,)), ((), ())), preferred_element_type=f32
    )
    out_pieces = out_part.astype(bf16).reshape(NY, NZ * NC, 32, hidden).swapaxes(0, 1)
    out_rows = exchange(out_pieces.reshape(NZ * NC, NY * 32, hidden), ZC_GROUPS)
    out_rows = jnp.sum(out_rows.astype(f32).reshape(NZ, NC, NY, 32, hidden), axis=0)
    grad_out = reduce_by_y(out_rows.swapaxes(0, 1), y_idx)
    up_proj = jnp.dot(wide_up, full_w_out, preferred_element_type=f32)
    act_grad = jax.vjp(gelu_tanh, pre_act)[1](up_proj)[0].astype(bf16)
    stat_part = jnp.sum(act_grad.astype(f32) * pre_act, axis=1) / inv_rms
    in_part = lax.dot_general(
        normed, act_grad, (((0,), (0,)), ((), ())), preferred_element_type=f32
    ).astype(bf16)
    in_rows = reduce_by_y(in_part.reshape(NY, NZ * NC * 32, hidden), y_idx)
    in_rows = exchange(in_rows.astype(bf16).reshape(NZ * NC, 32, hidden), ZC_GROUPS)
    grad_in = jnp.sum(in_rows.astype(f32).reshape(NZ, NC, 32, hidden), axis=0)

    normed_part = lax.dot_general(
        act_grad, full_w_in, (((1,), (1,)), ((), ())), preferred_element_type=f32
    )
    stat_high = stat_part.astype(bf16)
    stat_low = (stat_part - stat_high.astype(f32)).astype(bf16)
    lane = jnp.arange(128)[None, :]
    stat_cols = jnp.where(lane == 0, stat_high[:, None], stat_low[:, None])
    stat_cols = jnp.where(lane < 2, stat_cols, jnp.zeros((), bf16))
    sent = jnp.concatenate([normed_part[CAP:].astype(bf16), stat_cols[CAP:]], axis=1)
    got = swap_cores(sent)
    got = got.astype(f32)
    chip_part = normed_part[:CAP] + got[:, :width]
    chip_stat = stat_part[:CAP] + got[:, width] + got[:, width + 1]
    stat_high = chip_stat.astype(bf16)
    stat_low = (chip_stat - stat_high.astype(f32)).astype(bf16)
    stat_cols = jnp.where(lane == 0, stat_high[:, None], stat_low[:, None])
    stat_cols = jnp.where(lane < 2, stat_cols, jnp.zeros((), bf16))
    normed_grad = lax.dynamic_slice_in_dim(chip_part, x_idx * quarter, quarter, 1)
    row_stat = chip_stat
    for step in (1, 3, 2):
        piece = lax.dynamic_slice_in_dim(
            chip_part, ((x_idx + step) % NX) * quarter, quarter, 1
        ).astype(bf16)
        piece = jnp.concatenate([piece, stat_cols], axis=1)
        got = send_x(piece, step)
        got = got.astype(f32)
        normed_grad = normed_grad + got[:, :quarter]
        row_stat = row_stat + got[:, quarter] + got[:, quarter + 1]
    row_stat = row_stat / width
    own_rms = inv_rms[:CAP]
    pooled_grad = (
        up_grad.astype(f32)
        + own_rms[:, None] * normed_grad
        - pooled.astype(f32) * (own_rms**3 * row_stat)[:, None]
    ).astype(bf16)

    grad_spread = pooled_grad.astype(f32) * inv_length[:, None]
    last_spread = lax.dynamic_slice_in_dim(grad_spread, own_count - 1, 1, 0)
    tail_spread = lax.ppermute(last_spread, "seq", [(s, s + 1) for s in range(SEQ - 1)])
    grad_table = jnp.concatenate([grad_spread, tail_spread], axis=0)
    byte_act_grad = (byte_grads.astype(f32) + jnp.take(grad_table, slot_idx, axis=0)).astype(bf16)

    grad_scale = 1.0 / math.sqrt(SEQ * BAL)
    grad_in = grad_in.swapaxes(0, 1).reshape(32, NC * hidden) * grad_scale
    grad_out = grad_out.swapaxes(0, 1).reshape(32, NC * hidden) * grad_scale
    return (byte_act_grad, grad_in, grad_out)


def solution(mesh):
    in_specs = (P("seq", "mp"), P("seq", "mp"), P("seq"), P("seq", "mp"), P("seq", "mp"))
    out_specs = (P("seq", "mp"), P("seq", "mp"), P("seq", "mp"))

    return jax.shard_map(local, mesh=mesh, in_specs=in_specs, out_specs=out_specs, check_vma=False)
```

```python
import math

import jax
import jax.numpy as jnp
from jax import lax
from jax.experimental import pallas as pl
from jax.experimental.pallas import tpu as pltpu
from jax.sharding import PartitionSpec as P

BAL = 128
CAP = 224
NY, NZ, NC, NX = 4, 8, 2, 4
SEQ = NY * NZ * NC
epsilon = 1e-05
bf16 = jnp.bfloat16
f32 = jnp.float32


def seq_of(y, z, c):
    return ((y % NY) * NZ + (z % NZ)) * NC + c


def coords_of(s):
    return s // (NZ * NC), (s // NC) % NZ, s % NC


CORE_SWAP = [(s, s ^ 1) for s in range(SEQ)]
ZC_GROUPS = [[seq_of(y, z, c) for z in range(NZ) for c in range(NC)] for y in range(NY)]


def y_pairs(step):
    pairs = []
    for s in range(SEQ):
        y, z, c = coords_of(s)
        pairs.append((s, seq_of(y + step, z, c)))
    return pairs


def swap_cores(value):
    return lax.ppermute(value, "seq", CORE_SWAP)


def send_y(value, step):
    return lax.ppermute(value, "seq", y_pairs(step))


def send_x(value, step):
    return lax.ppermute(value, "mp", [(i, (i + step) % NX) for i in range(NX)])


def exchange(value, groups):
    return lax.all_to_all(value, "seq", 0, 0, axis_index_groups=groups, tiled=True)


def pick(value, index):
    return lax.dynamic_index_in_dim(value, index, 0, keepdims=False)


def gelu_tanh(values):
    return jax.nn.gelu(values, approximate=True)


def gather_by_y(column):
    return [column] + [send_y(column, step) for step in (1, 3, 2)]


def start_and_wait(pairs, sems):
    copies = [
        pltpu.make_async_copy(source, target, sems.at[n])
        for n, (source, target) in enumerate(pairs)
    ]
    for item in copies:
        item.start()
    for item in copies:
        item.wait()


STEPS = (0, 1, 3, 2)


def weight_kernel(at_ref, *refs):
    parts, (full_ref, sems) = refs[:4], refs[4:]
    pairs = [
        (part, full_ref.at[lax.rem(at_ref[1] + NY - step, NY)])
        for part, step in zip(parts, STEPS)
    ]
    start_and_wait(pairs, sems)


def rows_kernel(at_ref, own_ref, other_ref, pooled_ref, up_ref, sems):
    rows, quarter = own_ref.shape[2:]
    pairs = []
    for half, part in enumerate((own_ref, other_ref)):
        for n, step in enumerate(STEPS):
            x = lax.rem(at_ref[0] + NX - step, NX)
            where = (
                pl.ds(half * rows, rows),
                pl.ds(pl.multiple_of(x * quarter, quarter), quarter),
            )
            pairs.append((part.at[n, 0], pooled_ref.at[where]))
            pairs.append((part.at[n, 1], up_ref.at[where]))
    start_and_wait(pairs, sems)


def place(kernel, at, parts, shapes, n_copies):
    moved = sum(2 * math.prod(shape) for shape in shapes)
    return pl.pallas_call(
        kernel,
        out_shape=tuple(jax.ShapeDtypeStruct(shape, bf16) for shape in shapes),
        in_specs=[pl.BlockSpec(memory_space=pltpu.SMEM)]
        + [pl.BlockSpec(memory_space=pl.ANY)] * len(parts),
        out_specs=(pl.BlockSpec(memory_space=pltpu.VMEM),) * len(shapes),
        scratch_shapes=[pltpu.SemaphoreType.DMA((n_copies,))],
        cost_estimate=pl.CostEstimate(flops=0, bytes_accessed=2 * moved, transcendentals=0),
    )(at, *parts)


def place_weight(at, parts):
    depth, hidden = parts[0].shape
    (full,) = place(weight_kernel, at, parts, [(NY, depth, hidden)], 4)
    return full.reshape(NY * depth, hidden)


def place_rows(at, own_parts, other_parts):
    rows, quarter = own_parts.shape[2:]
    wide = (2 * rows, NX * quarter)
    return place(rows_kernel, at, [own_parts, other_parts], [wide, wide], 16)


def reduce_by_y(pieces, y_idx):
    total = pick(pieces, y_idx).astype(f32)
    for step in (1, 3, 2):
        got = send_y(pick(pieces, (y_idx + step) % NY).astype(bf16), step)
        total = total + got.astype(f32)
    return total


def local(byte_acts, byte_grads, row_of_byte, w_in, w_out):
    quarter = byte_acts.shape[1]
    width = quarter * NX
    hidden = w_in.shape[1] // NC
    shard_idx = lax.axis_index("seq")
    x_idx = lax.axis_index("mp")
    y_idx = shard_idx // (NZ * NC)

    def spread(weight):
        halves = weight.reshape(1, 32, NC, hidden).swapaxes(1, 2)
        copies = jnp.broadcast_to(halves, (NZ, NC, 32, hidden)).reshape(NZ * NC, 32, hidden)
        return exchange(copies, ZC_GROUPS).reshape(NZ * NC * 32, hidden)

    in_column = spread(w_in)
    in_parts = gather_by_y(in_column)
    out_column = spread(w_out)
    out_parts = gather_by_y(out_column)

    local_row = row_of_byte - shard_idx * CAP
    leading = local_row < 0
    slot_idx = jnp.where(leading, CAP, local_row)
    one_hot = (jnp.arange(CAP + 1, dtype=jnp.int32)[:, None] == slot_idx[None, :]).astype(bf16)
    act_sums = jnp.dot(one_hot, byte_acts, preferred_element_type=f32)
    grad_sums = jnp.dot(one_hot, byte_grads, preferred_element_type=f32)
    byte_counts = jnp.sum(one_hot.astype(f32), axis=1)
    own_count = jnp.max(jnp.where(leading, -1, local_row)) + 1
    frag = jnp.stack(
        [act_sums[CAP], grad_sums[CAP], jnp.broadcast_to(byte_counts[CAP], (quarter,))]
    )
    frag = lax.ppermute(frag, "seq", [(s, s - 1) for s in range(1, SEQ)])
    last_mark = (jnp.arange(CAP, dtype=jnp.int32) == own_count - 1).astype(f32)
    act_total = act_sums[:CAP] + last_mark[:, None] * frag[0][None, :]
    grad_total = grad_sums[:CAP] + last_mark[:, None] * frag[1][None, :]
    row_lengths = byte_counts[:CAP] + last_mark * frag[2, 0]
    inv_length = 1.0 / jnp.maximum(row_lengths, 1.0)
    pooled = (act_total * inv_length[:, None]).astype(bf16)
    up_grad = grad_total.astype(bf16)

    rows = jnp.stack([pooled, up_grad])
    own_parts = [rows] + [send_x(rows, step) for step in (1, 3, 2)]
    own_parts = jnp.stack(own_parts)
    other_parts = swap_cores(own_parts)
    at = jnp.stack([x_idx, y_idx]).astype(jnp.int32)
    wide_pooled, wide_up = place_rows(at, own_parts, other_parts)
    full_w_in = place_weight(at, in_parts)
    full_w_out = place_weight(at, out_parts)

    wide_f32 = wide_pooled.astype(f32)
    inv_rms = lax.rsqrt(jnp.mean(wide_f32 * wide_f32, axis=1) + epsilon)
    normed = (wide_f32 * inv_rms[:, None]).astype(bf16)
    pre_act = jnp.dot(normed, full_w_in, preferred_element_type=f32)
    activation = gelu_tanh(pre_act).astype(bf16)
    out_part = lax.dot_general(
        wide_up, activation, (((0,), (0,)), ((), ())), preferred_element_type=f32
    )
    out_part = out_part.astype(bf16)
    z_first = hidden - hidden // 4
    out_pieces = out_part[:, :z_first].reshape(NY, NZ * NC, 32, z_first).swapaxes(0, 1)
    out_rows = exchange(out_pieces.reshape(NZ * NC, NY * 32, z_first), ZC_GROUPS)
    out_rows = jnp.sum(out_rows.astype(f32).reshape(NZ, NC, NY, 32, z_first), axis=0)
    out_first = reduce_by_y(out_rows.swapaxes(0, 1), y_idx)
    out_second = reduce_by_y(
        out_part[:, z_first:].reshape(NY, NZ * NC * 32, hidden - z_first), y_idx
    )
    up_proj = jnp.dot(wide_up, full_w_out, preferred_element_type=f32)
    act_grad = jax.vjp(gelu_tanh, pre_act)[1](up_proj)[0].astype(bf16)
    stat_part = jnp.sum(act_grad.astype(f32) * pre_act, axis=1) / inv_rms
    in_part = lax.dot_general(
        normed, act_grad, (((0,), (0,)), ((), ())), preferred_element_type=f32
    ).astype(bf16)
    in_rows = reduce_by_y(in_part.reshape(NY, NZ * NC * 32, hidden), y_idx)
    in_rows = jnp.concatenate([in_rows, out_second], axis=1).astype(bf16)
    in_rows = exchange(in_rows.reshape(NZ * NC, 32, in_rows.shape[1]), ZC_GROUPS)
    in_rows = jnp.sum(in_rows.astype(f32).reshape(NZ, NC, 32, in_rows.shape[2]), axis=0)
    grad_in = in_rows[:, :, :hidden]
    grad_out = jnp.concatenate([out_first, in_rows[:, :, hidden:]], axis=2)

    normed_part = lax.dot_general(
        act_grad, full_w_in, (((1,), (1,)), ((), ())), preferred_element_type=f32
    )
    stat_high = stat_part.astype(bf16)
    stat_low = (stat_part - stat_high.astype(f32)).astype(bf16)
    lane = jnp.arange(128)[None, :]
    stat_cols = jnp.where(lane == 0, stat_high[:, None], stat_low[:, None])
    stat_cols = jnp.where(lane < 2, stat_cols, jnp.zeros((), bf16))
    sent = jnp.concatenate([normed_part[CAP:].astype(bf16), stat_cols[CAP:]], axis=1)
    got = swap_cores(sent)
    got = got.astype(f32)
    chip_part = normed_part[:CAP] + got[:, :width]
    chip_stat = stat_part[:CAP] + got[:, width] + got[:, width + 1]
    stat_high = chip_stat.astype(bf16)
    stat_low = (chip_stat - stat_high.astype(f32)).astype(bf16)
    stat_cols = jnp.where(lane == 0, stat_high[:, None], stat_low[:, None])
    stat_cols = jnp.where(lane < 2, stat_cols, jnp.zeros((), bf16))
    normed_grad = lax.dynamic_slice_in_dim(chip_part, x_idx * quarter, quarter, 1)
    row_stat = chip_stat
    for step in (1, 3, 2):
        piece = lax.dynamic_slice_in_dim(
            chip_part, ((x_idx + step) % NX) * quarter, quarter, 1
        ).astype(bf16)
        piece = jnp.concatenate([piece, stat_cols], axis=1)
        got = send_x(piece, step)
        got = got.astype(f32)
        normed_grad = normed_grad + got[:, :quarter]
        row_stat = row_stat + got[:, quarter] + got[:, quarter + 1]
    row_stat = row_stat / width
    own_rms = inv_rms[:CAP]
    pooled_grad = (
        up_grad.astype(f32)
        + own_rms[:, None] * normed_grad
        - pooled.astype(f32) * (own_rms**3 * row_stat)[:, None]
    ).astype(bf16)

    grad_spread = pooled_grad.astype(f32) * inv_length[:, None]
    last_spread = lax.dynamic_slice_in_dim(grad_spread, own_count - 1, 1, 0)
    tail_spread = lax.ppermute(last_spread, "seq", [(s, s + 1) for s in range(SEQ - 1)])
    grad_table = jnp.concatenate([grad_spread, tail_spread], axis=0)
    byte_act_grad = (byte_grads.astype(f32) + jnp.take(grad_table, slot_idx, axis=0)).astype(bf16)

    grad_scale = 1.0 / math.sqrt(SEQ * BAL)
    grad_in = grad_in.swapaxes(0, 1).reshape(32, NC * hidden) * grad_scale
    grad_out = grad_out.swapaxes(0, 1).reshape(32, NC * hidden) * grad_scale
    return (byte_act_grad, grad_in, grad_out)


def solution(mesh):
    in_specs = (P("seq", "mp"), P("seq", "mp"), P("seq"), P("seq", "mp"), P("seq", "mp"))
    out_specs = (P("seq", "mp"), P("seq", "mp"), P("seq", "mp"))

    return jax.shard_map(local, mesh=mesh, in_specs=in_specs, out_specs=out_specs, check_vma=False)
```

```python
import math

import jax
import jax.numpy as jnp
from jax import lax
from jax.experimental import pallas as pl
from jax.experimental.pallas import tpu as pltpu
from jax.sharding import PartitionSpec as P

BAL = 128
CAP = 224
NY, NZ, NC, NX = 4, 8, 2, 4
SEQ = NY * NZ * NC
epsilon = 1e-05
bf16 = jnp.bfloat16
f32 = jnp.float32


def seq_of(y, z, c):
    return ((y % NY) * NZ + (z % NZ)) * NC + c


def coords_of(s):
    return s // (NZ * NC), (s // NC) % NZ, s % NC


CORE_SWAP = [(s, s ^ 1) for s in range(SEQ)]
ZC_GROUPS = [[seq_of(y, z, c) for z in range(NZ) for c in range(NC)] for y in range(NY)]


def y_pairs(step):
    pairs = []
    for s in range(SEQ):
        y, z, c = coords_of(s)
        pairs.append((s, seq_of(y + step, z, c)))
    return pairs


def swap_cores(value):
    return lax.ppermute(value, "seq", CORE_SWAP)


def send_y(value, step):
    return lax.ppermute(value, "seq", y_pairs(step))


def send_x(value, step):
    return lax.ppermute(value, "mp", [(i, (i + step) % NX) for i in range(NX)])


def exchange(value, groups):
    return lax.all_to_all(value, "seq", 0, 0, axis_index_groups=groups, tiled=True)


def pick(value, index):
    return lax.dynamic_index_in_dim(value, index, 0, keepdims=False)


def gelu_tanh(values):
    return jax.nn.gelu(values, approximate=True)


def gather_by_y(column):
    return [column] + [send_y(column, step) for step in (1, 3, 2)]


STEPS = (0, 1, 3, 2)
CHUNK = 64
MIB = 1 << 20


def copies_of(pairs, sems):
    return [
        pltpu.make_async_copy(source, target, sems.at[n])
        for n, (source, target) in enumerate(pairs)
    ]


def weight_copies(at_ref, parts, full_ref, sems):
    return copies_of(
        [
            (part, full_ref.at[lax.rem(at_ref[1] + NY - step, NY)])
            for part, step in zip(parts, STEPS)
        ],
        sems,
    )


def norm_kernel(at_ref, own_ref, other_ref, normed_ref, up_ref, rms_ref, pooled_ref, sems):
    rows, quarter = own_ref.shape[2:]
    pairs = []
    for half, part in enumerate((own_ref, other_ref)):
        for n, step in enumerate(STEPS):
            x = lax.rem(at_ref[0] + NX - step, NX)
            where = (
                pl.ds(half * rows, rows),
                pl.ds(pl.multiple_of(x * quarter, quarter), quarter),
            )
            pairs.append((part.at[n, 0], pooled_ref.at[where]))
            pairs.append((part.at[n, 1], up_ref.at[where]))
    copies = copies_of(pairs, sems)
    for item in copies:
        item.start()
    for item in copies:
        item.wait()

    def norm_rows(i, carry):
        at = pl.ds(pl.multiple_of(i * CHUNK, CHUNK), CHUNK)
        values = pooled_ref[at, :].astype(f32)
        rms = lax.rsqrt(jnp.mean(values * values, axis=1, keepdims=True) + epsilon)
        normed_ref[at, :] = (values * rms).astype(bf16)
        rms_ref[at, :] = jnp.broadcast_to(rms, (CHUNK, rms_ref.shape[1]))
        return carry

    lax.fori_loop(0, pooled_ref.shape[0] // CHUNK, norm_rows, 0)


def act_kernel(at_ref, *refs):
    parts, (normed_ref, up_ref, w_in_ref, pre_ref, out_ref, act_ref, sems) = refs[:4], refs[4:]
    copies = weight_copies(at_ref, parts, w_in_ref, sems)
    for item in copies:
        item.start()
    for item in copies:
        item.wait()
    rows, width = normed_ref.shape
    depth, hidden = w_in_ref.shape[1:]
    for n in range(0, hidden, 256):
        weight = w_in_ref[:, :, n : n + 256].reshape(width, 256)
        pre_ref[:, n : n + 256] = jnp.dot(normed_ref[...], weight, preferred_element_type=f32)

    def act_rows(i, carry):
        at = pl.ds(pl.multiple_of(i * CHUNK, CHUNK), CHUNK)
        act_ref[at, :] = gelu_tanh(pre_ref[at, :]).astype(bf16)
        return carry

    lax.fori_loop(0, rows // CHUNK, act_rows, 0)
    for y in range(NY):
        part = lax.dot_general(
            up_ref[:, y * depth : (y + 1) * depth],
            act_ref[...],
            (((0,), (0,)), ((), ())),
            preferred_element_type=f32,
        ).astype(bf16)
        out_ref[:, y * 32 : (y + 1) * 32, :] = part.reshape(NZ * NC, 32, hidden)


GELU_K = math.sqrt(2.0 / math.pi)


def gelu_slope(v):
    square = v * v
    t = jnp.tanh(GELU_K * (v + 0.044715 * (square * v)))
    inner = GELU_K * (1.0 + 3 * 0.044715 * square)
    return 0.5 * (1.0 + t) + 0.5 * v * ((1.0 - t * t) * inner)


def grad_kernel(at_ref, *refs):
    parts, refs = refs[:4], refs[4:]
    normed_ref, up_ref, w_in_ref, pre_ref, rms_ref = refs[:5]
    in_refs, (own_ref, sent_ref, stat_ref) = refs[5:9], refs[9:12]
    w_out_ref, proj_ref, grad_ref, row_ref, sems = refs[12:]
    copies = weight_copies(at_ref, parts, w_out_ref, sems)
    for item in copies:
        item.start()
    for item in copies:
        item.wait()
    rows, width = normed_ref.shape
    depth, hidden = w_in_ref.shape[1:]
    half = rows // 2
    for n in range(0, hidden, 256):
        weight = w_out_ref[:, :, n : n + 256].reshape(width, 256)
        proj_ref[:, n : n + 256] = jnp.dot(up_ref[...], weight, preferred_element_type=f32)

    def grad_rows(i, carry):
        at = pl.ds(pl.multiple_of(i * CHUNK, CHUNK), CHUNK)
        pre = pre_ref[at, :]
        grad = (proj_ref[at, :] * gelu_slope(pre)).astype(bf16)
        grad_ref[at, :] = grad
        stat = jnp.sum(grad.astype(f32) * pre, axis=1, keepdims=True)
        row_ref[at, :] = jnp.broadcast_to(stat, (CHUNK, 128)) / rms_ref[at, :]
        return carry

    lax.fori_loop(0, rows // CHUNK, grad_rows, 0)
    for step, in_ref in zip(STEPS, in_refs):
        y = lax.rem(at_ref[1] + step, NY)
        block = normed_ref[:, pl.ds(pl.multiple_of(y * depth, depth), depth)]
        in_ref[...] = lax.dot_general(
            block, grad_ref[...], (((0,), (0,)), ((), ())), preferred_element_type=f32
        ).astype(bf16)
    for n in range(NY):
        part = lax.dot_general(
            grad_ref[...], w_in_ref[n], (((1,), (1,)), ((), ())), preferred_element_type=f32
        )
        own_ref[:, n * depth : (n + 1) * depth] = part[:half]
        sent_ref[:, n * depth : (n + 1) * depth] = part[half:].astype(bf16)
    stat = row_ref[half:, :]
    high = stat.astype(bf16).astype(f32)
    lane = lax.broadcasted_iota(jnp.int32, (half, 128), 1)
    low = jnp.where(lane == 1, stat - high, 0.0)
    sent_ref[:, width:] = jnp.where(lane == 0, high, low).astype(bf16)
    stat_ref[...] = row_ref[:half, :]


def call(kernel, at, far, near, outs, scratch, n_copies, limit, flops):
    outs = [jax.ShapeDtypeStruct(shape, dtype) for shape, dtype in outs]
    moved = sum(v.size * v.dtype.itemsize for v in [*far, *near, *outs])
    return pl.pallas_call(
        kernel,
        out_shape=tuple(outs),
        in_specs=[pl.BlockSpec(memory_space=pltpu.SMEM)]
        + [pl.BlockSpec(memory_space=pl.ANY)] * len(far)
        + [pl.BlockSpec(memory_space=pltpu.VMEM)] * len(near),
        out_specs=(pl.BlockSpec(memory_space=pltpu.VMEM),) * len(outs),
        scratch_shapes=[pltpu.VMEM(shape, dtype) for shape, dtype in scratch]
        + [pltpu.SemaphoreType.DMA((n_copies,))],
        cost_estimate=pl.CostEstimate(flops=flops, bytes_accessed=moved, transcendentals=0),
        compiler_params=pltpu.CompilerParams(vmem_limit_bytes=limit * MIB),
    )(at, *far, *near)


def reduce_sent(own, pieces):
    total = own.astype(f32)
    for piece, step in zip(pieces, STEPS[1:]):
        total = total + send_y(piece, step).astype(f32)
    return total


def reduce_by_y(pieces, y_idx):
    total = pick(pieces, y_idx).astype(f32)
    for step in (1, 3, 2):
        got = send_y(pick(pieces, (y_idx + step) % NY).astype(bf16), step)
        total = total + got.astype(f32)
    return total


def local(byte_acts, byte_grads, row_of_byte, w_in, w_out):
    quarter = byte_acts.shape[1]
    width = quarter * NX
    hidden = w_in.shape[1] // NC
    shard_idx = lax.axis_index("seq")
    x_idx = lax.axis_index("mp")
    y_idx = shard_idx // (NZ * NC)

    def spread(weight):
        halves = weight.reshape(1, 32, NC, hidden).swapaxes(1, 2)
        copies = jnp.broadcast_to(halves, (NZ, NC, 32, hidden)).reshape(NZ * NC, 32, hidden)
        return exchange(copies, ZC_GROUPS).reshape(NZ * NC * 32, hidden)

    in_column = spread(w_in)
    in_parts = gather_by_y(in_column)
    out_column = spread(w_out)
    out_parts = gather_by_y(out_column)

    local_row = row_of_byte - shard_idx * CAP
    leading = local_row < 0
    slot_idx = jnp.where(leading, CAP, local_row)
    one_hot = (jnp.arange(CAP + 1, dtype=jnp.int32)[:, None] == slot_idx[None, :]).astype(bf16)
    act_sums = jnp.dot(one_hot, byte_acts, preferred_element_type=f32)
    grad_sums = jnp.dot(one_hot, byte_grads, preferred_element_type=f32)
    byte_counts = jnp.sum(one_hot.astype(f32), axis=1)
    own_count = jnp.max(jnp.where(leading, -1, local_row)) + 1
    frag = jnp.stack(
        [act_sums[CAP], grad_sums[CAP], jnp.broadcast_to(byte_counts[CAP], (quarter,))]
    )
    frag = lax.ppermute(frag, "seq", [(s, s - 1) for s in range(1, SEQ)])
    last_mark = (jnp.arange(CAP, dtype=jnp.int32) == own_count - 1).astype(f32)
    act_total = act_sums[:CAP] + last_mark[:, None] * frag[0][None, :]
    grad_total = grad_sums[:CAP] + last_mark[:, None] * frag[1][None, :]
    row_lengths = byte_counts[:CAP] + last_mark * frag[2, 0]
    inv_length = 1.0 / jnp.maximum(row_lengths, 1.0)
    pooled = (act_total * inv_length[:, None]).astype(bf16)
    up_grad = grad_total.astype(bf16)

    rows = jnp.stack([pooled, up_grad])
    own_parts = [rows] + [send_x(rows, step) for step in (1, 3, 2)]
    own_parts = jnp.stack(own_parts)
    other_parts = swap_cores(own_parts)
    at = jnp.stack([x_idx, y_idx]).astype(jnp.int32)
    rows_all, depth = 2 * CAP, width // NY
    normed, wide_up, wide_rms = call(
        norm_kernel,
        at,
        [own_parts, other_parts],
        [],
        [((rows_all, width), bf16), ((rows_all, width), bf16), ((rows_all, 128), f32)],
        [((rows_all, width), bf16)],
        16,
        16,
        0,
    )
    product = 2 * rows_all * width * hidden
    full_w_in, pre_act, out_pieces = call(
        act_kernel,
        at,
        in_parts,
        [normed, wide_up],
        [
            ((NY, depth, hidden), bf16),
            ((rows_all, hidden), f32),
            ((NZ * NC, NY * 32, hidden), bf16),
        ],
        [((rows_all, hidden), bf16)],
        4,
        24,
        2 * product,
    )
    out_rows = exchange(out_pieces, ZC_GROUPS)
    out_rows = jnp.sum(out_rows.astype(f32).reshape(NZ, NC, NY, 32, hidden), axis=0)
    grad_out = reduce_by_y(out_rows.swapaxes(0, 1), y_idx)
    *in_pieces, own_part, sent, own_stat = call(
        grad_kernel,
        at,
        out_parts,
        [normed, wide_up, full_w_in, pre_act, wide_rms],
        [((depth, hidden), bf16)] * NY
        + [((CAP, width), f32), ((CAP, width + 128), bf16), ((CAP, 128), f32)],
        [
            ((NY, depth, hidden), bf16),
            ((rows_all, hidden), f32),
            ((rows_all, hidden), bf16),
            ((rows_all, 128), f32),
        ],
        4,
        32,
        3 * product,
    )
    in_rows = reduce_sent(in_pieces[0], in_pieces[1:])
    in_rows = exchange(in_rows.astype(bf16).reshape(NZ * NC, 32, hidden), ZC_GROUPS)
    grad_in = jnp.sum(in_rows.astype(f32).reshape(NZ, NC, 32, hidden), axis=0)

    got = swap_cores(sent)
    got = got.astype(f32)
    chip_part = own_part + got[:, :width]
    chip_stat = own_stat[:, 0] + got[:, width] + got[:, width + 1]
    lane = jnp.arange(128)[None, :]
    stat_high = chip_stat.astype(bf16)
    stat_low = (chip_stat - stat_high.astype(f32)).astype(bf16)
    stat_cols = jnp.where(lane == 0, stat_high[:, None], stat_low[:, None])
    stat_cols = jnp.where(lane < 2, stat_cols, jnp.zeros((), bf16))
    normed_grad = lax.dynamic_slice_in_dim(chip_part, x_idx * quarter, quarter, 1)
    row_stat = chip_stat
    for step in (1, 3, 2):
        piece = lax.dynamic_slice_in_dim(
            chip_part, ((x_idx + step) % NX) * quarter, quarter, 1
        ).astype(bf16)
        piece = jnp.concatenate([piece, stat_cols], axis=1)
        got = send_x(piece, step)
        got = got.astype(f32)
        normed_grad = normed_grad + got[:, :quarter]
        row_stat = row_stat + got[:, quarter] + got[:, quarter + 1]
    row_stat = row_stat / width
    own_rms = wide_rms[:CAP, 0]
    pooled_grad = (
        up_grad.astype(f32)
        + own_rms[:, None] * normed_grad
        - pooled.astype(f32) * (own_rms**3 * row_stat)[:, None]
    ).astype(bf16)

    grad_spread = pooled_grad.astype(f32) * inv_length[:, None]
    last_spread = lax.dynamic_slice_in_dim(grad_spread, own_count - 1, 1, 0)
    tail_spread = lax.ppermute(last_spread, "seq", [(s, s + 1) for s in range(SEQ - 1)])
    grad_table = jnp.concatenate([grad_spread, tail_spread], axis=0)
    byte_act_grad = (byte_grads.astype(f32) + jnp.take(grad_table, slot_idx, axis=0)).astype(bf16)

    grad_scale = 1.0 / math.sqrt(SEQ * BAL)
    grad_in = grad_in.swapaxes(0, 1).reshape(32, NC * hidden) * grad_scale
    grad_out = grad_out.swapaxes(0, 1).reshape(32, NC * hidden) * grad_scale
    return (byte_act_grad, grad_in, grad_out)


def solution(mesh):
    in_specs = (P("seq", "mp"), P("seq", "mp"), P("seq"), P("seq", "mp"), P("seq", "mp"))
    out_specs = (P("seq", "mp"), P("seq", "mp"), P("seq", "mp"))

    return jax.shard_map(local, mesh=mesh, in_specs=in_specs, out_specs=out_specs, check_vma=False)
```

```python
import math

import jax
import jax.numpy as jnp
from jax import lax
from jax.experimental import pallas as pl
from jax.experimental.pallas import tpu as pltpu
from jax.sharding import PartitionSpec as P

BAL = 128
CAP = 224
NY, NZ, NC, NX = 4, 8, 2, 4
SEQ = NY * NZ * NC
epsilon = 1e-05
bf16 = jnp.bfloat16
f32 = jnp.float32


def seq_of(y, z, c):
    return ((y % NY) * NZ + (z % NZ)) * NC + c


def coords_of(s):
    return s // (NZ * NC), (s // NC) % NZ, s % NC


CORE_SWAP = [(s, s ^ 1) for s in range(SEQ)]
ZC_GROUPS = [[seq_of(y, z, c) for z in range(NZ) for c in range(NC)] for y in range(NY)]


def y_pairs(step):
    pairs = []
    for s in range(SEQ):
        y, z, c = coords_of(s)
        pairs.append((s, seq_of(y + step, z, c)))
    return pairs


def swap_cores(value):
    return lax.ppermute(value, "seq", CORE_SWAP)


def send_y(value, step):
    return lax.ppermute(value, "seq", y_pairs(step))


def send_x(value, step):
    return lax.ppermute(value, "mp", [(i, (i + step) % NX) for i in range(NX)])


def exchange(value, groups):
    return lax.all_to_all(value, "seq", 0, 0, axis_index_groups=groups, tiled=True)


def pick(value, index):
    return lax.dynamic_index_in_dim(value, index, 0, keepdims=False)


def gelu_tanh(values):
    return jax.nn.gelu(values, approximate=True)


def gather_by_y(column):
    return [column] + [send_y(column, step) for step in (1, 3, 2)]


STEPS = (0, 1, 3, 2)
CHUNK = 64


class Copies:
    def __init__(self, sems):
        self.sems, self.used = sems, 0

    def start(self, pairs):
        started = []
        for source, target in pairs:
            started.append(pltpu.make_async_copy(source, target, self.sems.at[self.used]))
            self.used += 1
            started[-1].start()
        return started


def wait(copies):
    for item in copies:
        item.wait()


def weight_pairs(at_ref, parts, full_ref):
    return [
        (part, full_ref.at[lax.rem(at_ref[1] + NY - step, NY)])
        for part, step in zip(parts, STEPS)
    ]


def norm_kernel(
    at_ref, own_ref, other_ref, normed_out, up_out, rms_out,
    pooled_ref, normed_ref, up_ref, rms_ref, sems,
):
    move = Copies(sems)
    rows, quarter = own_ref.shape[2:]
    places = []
    for half, part in enumerate((own_ref, other_ref)):
        for n, step in enumerate(STEPS):
            x = lax.rem(at_ref[0] + NX - step, NX)
            where = (
                pl.ds(half * rows, rows),
                pl.ds(pl.multiple_of(x * quarter, quarter), quarter),
            )
            places.append((part.at[n], where))
    pooled = move.start([(part.at[0], pooled_ref.at[where]) for part, where in places])
    ups = move.start([(part.at[1], up_ref.at[where]) for part, where in places])
    wait(pooled)

    def norm_rows(i, carry):
        at = pl.ds(pl.multiple_of(i * CHUNK, CHUNK), CHUNK)
        values = pooled_ref[at, :].astype(f32)
        rms = lax.rsqrt(jnp.mean(values * values, axis=1, keepdims=True) + epsilon)
        normed_ref[at, :] = (values * rms).astype(bf16)
        rms_ref[at, :] = jnp.broadcast_to(rms, (CHUNK, rms_ref.shape[1]))
        return carry

    lax.fori_loop(0, pooled_ref.shape[0] // CHUNK, norm_rows, 0)
    gone = move.start([(normed_ref, normed_out), (rms_ref, rms_out)])
    wait(ups)
    wait(gone + move.start([(up_ref, up_out)]))


def act_kernel(at_ref, *refs):
    parts, (normed_in, up_in, pre_out, out_out), refs = refs[:4], refs[4:8], refs[8:]
    normed_ref, up_ref, w_in_ref, pre_ref, act_ref, out_ref, sems = refs
    move = Copies(sems)
    first = move.start([(normed_in, normed_ref)] + weight_pairs(at_ref, parts, w_in_ref))
    second = move.start([(up_in, up_ref)])
    wait(first)
    rows, width = normed_ref.shape
    depth, hidden = w_in_ref.shape[1:]
    for n in range(0, hidden, 256):
        weight = w_in_ref[:, :, n : n + 256].reshape(width, 256)
        pre_ref[:, n : n + 256] = jnp.dot(normed_ref[...], weight, preferred_element_type=f32)
    gone = move.start([(pre_ref, pre_out)])

    def act_rows(i, carry):
        at = pl.ds(pl.multiple_of(i * CHUNK, CHUNK), CHUNK)
        act_ref[at, :] = gelu_tanh(pre_ref[at, :]).astype(bf16)
        return carry

    lax.fori_loop(0, rows // CHUNK, act_rows, 0)
    wait(second)
    for y in range(NY):
        part = lax.dot_general(
            up_ref[:, y * depth : (y + 1) * depth],
            act_ref[...],
            (((0,), (0,)), ((), ())),
            preferred_element_type=f32,
        ).astype(bf16)
        out_ref[y] = part.reshape(NZ * NC, 32, hidden)
        gone += move.start([(out_ref.at[y], out_out.at[:, pl.ds(y * 32, 32), :])])
    wait(gone)


GELU_K = math.sqrt(2.0 / math.pi)


def gelu_slope(v):
    square = v * v
    t = jnp.tanh(GELU_K * (v + 0.044715 * (square * v)))
    inner = GELU_K * (1.0 + 3 * 0.044715 * square)
    return 0.5 * (1.0 + t) + 0.5 * v * ((1.0 - t * t) * inner)


def grad_kernel(at_ref, *refs):
    out_parts, in_parts, refs = refs[:4], refs[4:8], refs[8:]
    normed_in, up_in, pre_in, rms_in = refs[:4]
    in_outs, (own_out, sent_out, stat_ref), refs = refs[4:8], refs[8:11], refs[11:]
    normed_ref, up_ref, pre_ref, rms_ref, w_out_ref, w_in_ref = refs[:6]
    proj_ref, grad_ref, row_ref, in_ref, own_ref, sent_ref, sems = refs[6:]
    move = Copies(sems)
    first = move.start([(up_in, up_ref)] + weight_pairs(at_ref, out_parts, w_out_ref))
    second = move.start([(pre_in, pre_ref), (rms_in, rms_ref)])
    third = move.start([(normed_in, normed_ref)])
    fourth = move.start(weight_pairs(at_ref, in_parts, w_in_ref))
    wait(first)
    rows, width = normed_ref.shape
    depth, hidden = w_in_ref.shape[1:]
    half = rows // 2
    for n in range(0, hidden, 256):
        weight = w_out_ref[:, :, n : n + 256].reshape(width, 256)
        proj_ref[:, n : n + 256] = jnp.dot(up_ref[...], weight, preferred_element_type=f32)
    wait(second)

    def grad_rows(i, carry):
        at = pl.ds(pl.multiple_of(i * CHUNK, CHUNK), CHUNK)
        pre = pre_ref[at, :]
        grad = (proj_ref[at, :] * gelu_slope(pre)).astype(bf16)
        grad_ref[at, :] = grad
        stat = jnp.sum(grad.astype(f32) * pre, axis=1, keepdims=True)
        row_ref[at, :] = jnp.broadcast_to(stat, (CHUNK, 128)) / rms_ref[at, :]
        return carry

    lax.fori_loop(0, rows // CHUNK, grad_rows, 0)
    wait(third)
    gone = []
    for n, step in enumerate(STEPS):
        y = lax.rem(at_ref[1] + step, NY)
        block = normed_ref[:, pl.ds(pl.multiple_of(y * depth, depth), depth)]
        in_ref[n] = lax.dot_general(
            block, grad_ref[...], (((0,), (0,)), ((), ())), preferred_element_type=f32
        ).astype(bf16)
        gone += move.start([(in_ref.at[n], in_outs[n])])
    wait(fourth)
    for n in range(NY):
        part = lax.dot_general(
            grad_ref[...], w_in_ref[n], (((1,), (1,)), ((), ())), preferred_element_type=f32
        )
        own_ref[:, n * depth : (n + 1) * depth] = part[:half]
        sent_ref[:, n * depth : (n + 1) * depth] = part[half:].astype(bf16)
    stat = row_ref[half:, :]
    high = stat.astype(bf16).astype(f32)
    lane = lax.broadcasted_iota(jnp.int32, (half, 128), 1)
    low = jnp.where(lane == 1, stat - high, 0.0)
    sent_ref[:, width:] = jnp.where(lane == 0, high, low).astype(bf16)
    stat_ref[...] = row_ref[:half, :]
    wait(gone + move.start([(own_ref, own_out), (sent_ref, sent_out)]))


def call(kernel, at, far, outs, scratch, n_copies, flops, near=0):
    outs = [jax.ShapeDtypeStruct(shape, dtype) for shape, dtype in outs]
    moved = sum(v.size * v.dtype.itemsize for v in [*far, *outs])
    return pl.pallas_call(
        kernel,
        out_shape=tuple(outs),
        in_specs=[pl.BlockSpec(memory_space=pltpu.SMEM)]
        + [pl.BlockSpec(memory_space=pl.ANY)] * len(far),
        out_specs=(pl.BlockSpec(memory_space=pltpu.HBM),) * (len(outs) - near)
        + (pl.BlockSpec(memory_space=pltpu.VMEM),) * near,
        scratch_shapes=[pltpu.VMEM(shape, dtype) for shape, dtype in scratch]
        + [pltpu.SemaphoreType.DMA((n_copies,))],
        cost_estimate=pl.CostEstimate(flops=flops, bytes_accessed=moved, transcendentals=0),
    )(at, *far)


def reduce_sent(own, pieces):
    total = own.astype(f32)
    for piece, step in zip(pieces, STEPS[1:]):
        total = total + send_y(piece, step).astype(f32)
    return total


def reduce_by_y(pieces, y_idx):
    total = pick(pieces, y_idx).astype(f32)
    for step in (1, 3, 2):
        got = send_y(pick(pieces, (y_idx + step) % NY).astype(bf16), step)
        total = total + got.astype(f32)
    return total


def local(byte_acts, byte_grads, row_of_byte, w_in, w_out):
    quarter = byte_acts.shape[1]
    width = quarter * NX
    hidden = w_in.shape[1] // NC
    shard_idx = lax.axis_index("seq")
    x_idx = lax.axis_index("mp")
    y_idx = shard_idx // (NZ * NC)

    def spread(weight):
        halves = weight.reshape(1, 32, NC, hidden).swapaxes(1, 2)
        copies = jnp.broadcast_to(halves, (NZ, NC, 32, hidden)).reshape(NZ * NC, 32, hidden)
        return exchange(copies, ZC_GROUPS).reshape(NZ * NC * 32, hidden)

    in_column = spread(w_in)
    in_parts = gather_by_y(in_column)
    out_column = spread(w_out)
    out_parts = gather_by_y(out_column)

    local_row = row_of_byte - shard_idx * CAP
    leading = local_row < 0
    slot_idx = jnp.where(leading, CAP, local_row)
    one_hot = (jnp.arange(CAP + 1, dtype=jnp.int32)[:, None] == slot_idx[None, :]).astype(bf16)
    act_sums = jnp.dot(one_hot, byte_acts, preferred_element_type=f32)
    grad_sums = jnp.dot(one_hot, byte_grads, preferred_element_type=f32)
    byte_counts = jnp.sum(one_hot.astype(f32), axis=1)
    own_count = jnp.max(jnp.where(leading, -1, local_row)) + 1
    frag = jnp.stack(
        [act_sums[CAP], grad_sums[CAP], jnp.broadcast_to(byte_counts[CAP], (quarter,))]
    )
    frag = lax.ppermute(frag, "seq", [(s, s - 1) for s in range(1, SEQ)])
    last_mark = (jnp.arange(CAP, dtype=jnp.int32) == own_count - 1).astype(f32)
    act_total = act_sums[:CAP] + last_mark[:, None] * frag[0][None, :]
    grad_total = grad_sums[:CAP] + last_mark[:, None] * frag[1][None, :]
    row_lengths = byte_counts[:CAP] + last_mark * frag[2, 0]
    inv_length = 1.0 / jnp.maximum(row_lengths, 1.0)
    pooled = (act_total * inv_length[:, None]).astype(bf16)
    up_grad = grad_total.astype(bf16)

    rows = jnp.stack([pooled, up_grad])
    own_parts = [rows] + [send_x(rows, step) for step in (1, 3, 2)]
    own_parts = jnp.stack(own_parts)
    other_parts = swap_cores(own_parts)
    at = jnp.stack([x_idx, y_idx]).astype(jnp.int32)
    rows_all, depth = 2 * CAP, width // NY
    wide, thin = ((rows_all, width), bf16), ((rows_all, 128), f32)
    square, weight = ((rows_all, hidden), f32), ((NY, depth, hidden), bf16)
    normed, wide_up, wide_rms = call(
        norm_kernel,
        at,
        [own_parts, other_parts],
        [wide, wide, thin],
        [wide, wide, wide, thin],
        19,
        0,
    )
    product = 2 * rows_all * width * hidden
    pre_act, out_pieces = call(
        act_kernel,
        at,
        [*in_parts, normed, wide_up],
        [square, ((NZ * NC, NY * 32, hidden), bf16)],
        [wide, wide, weight, square, ((rows_all, hidden), bf16), ((NY, NZ * NC, 32, hidden), bf16)],
        11,
        2 * product,
    )
    out_rows = exchange(out_pieces, ZC_GROUPS)
    out_rows = jnp.sum(out_rows.astype(f32).reshape(NZ, NC, NY, 32, hidden), axis=0)
    grad_out = reduce_by_y(out_rows.swapaxes(0, 1), y_idx)
    *in_pieces, own_part, sent, own_stat = call(
        grad_kernel,
        at,
        [*out_parts, *in_parts, normed, wide_up, pre_act, wide_rms],
        [((depth, hidden), bf16)] * NY
        + [((CAP, width), f32), ((CAP, width + 128), bf16), ((CAP, 128), f32)],
        [
            wide,
            wide,
            square,
            thin,
            weight,
            weight,
            square,
            ((rows_all, hidden), bf16),
            thin,
            weight,
            ((CAP, width), f32),
            ((CAP, width + 128), bf16),
        ],
        18,
        3 * product,
        near=1,
    )
    in_rows = reduce_sent(in_pieces[0], in_pieces[1:])
    in_rows = exchange(in_rows.astype(bf16).reshape(NZ * NC, 32, hidden), ZC_GROUPS)
    grad_in = jnp.sum(in_rows.astype(f32).reshape(NZ, NC, 32, hidden), axis=0)

    got = swap_cores(sent)
    got = got.astype(f32)
    chip_part = own_part + got[:, :width]
    chip_stat = own_stat[:, 0] + got[:, width] + got[:, width + 1]
    lane = jnp.arange(128)[None, :]
    stat_high = chip_stat.astype(bf16)
    stat_low = (chip_stat - stat_high.astype(f32)).astype(bf16)
    stat_cols = jnp.where(lane == 0, stat_high[:, None], stat_low[:, None])
    stat_cols = jnp.where(lane < 2, stat_cols, jnp.zeros((), bf16))
    normed_grad = lax.dynamic_slice_in_dim(chip_part, x_idx * quarter, quarter, 1)
    row_stat = chip_stat
    for step in (1, 3, 2):
        piece = lax.dynamic_slice_in_dim(
            chip_part, ((x_idx + step) % NX) * quarter, quarter, 1
        ).astype(bf16)
        piece = jnp.concatenate([piece, stat_cols], axis=1)
        got = send_x(piece, step)
        got = got.astype(f32)
        normed_grad = normed_grad + got[:, :quarter]
        row_stat = row_stat + got[:, quarter] + got[:, quarter + 1]
    row_stat = row_stat / width
    own_rms = wide_rms[:CAP, 0]
    pooled_grad = (
        up_grad.astype(f32)
        + own_rms[:, None] * normed_grad
        - pooled.astype(f32) * (own_rms**3 * row_stat)[:, None]
    ).astype(bf16)

    grad_spread = pooled_grad.astype(f32) * inv_length[:, None]
    last_spread = lax.dynamic_slice_in_dim(grad_spread, own_count - 1, 1, 0)
    tail_spread = lax.ppermute(last_spread, "seq", [(s, s + 1) for s in range(SEQ - 1)])
    grad_table = jnp.concatenate([grad_spread, tail_spread], axis=0)
    byte_act_grad = (byte_grads.astype(f32) + jnp.take(grad_table, slot_idx, axis=0)).astype(bf16)

    grad_scale = 1.0 / math.sqrt(SEQ * BAL)
    grad_in = grad_in.swapaxes(0, 1).reshape(32, NC * hidden) * grad_scale
    grad_out = grad_out.swapaxes(0, 1).reshape(32, NC * hidden) * grad_scale
    return (byte_act_grad, grad_in, grad_out)


def solution(mesh):
    in_specs = (P("seq", "mp"), P("seq", "mp"), P("seq"), P("seq", "mp"), P("seq", "mp"))
    out_specs = (P("seq", "mp"), P("seq", "mp"), P("seq", "mp"))

    return jax.shard_map(local, mesh=mesh, in_specs=in_specs, out_specs=out_specs, check_vma=False)
```

```python
import math

import jax
import jax.numpy as jnp
from jax import lax
from jax.experimental import pallas as pl
from jax.experimental.pallas import tpu as pltpu
from jax.sharding import PartitionSpec as P

BAL = 128
CAP = 224
NY, NZ, NC, NX = 4, 8, 2, 4
SEQ = NY * NZ * NC
epsilon = 1e-05
bf16 = jnp.bfloat16
f32 = jnp.float32


def seq_of(y, z, c):
    return ((y % NY) * NZ + (z % NZ)) * NC + c


def coords_of(s):
    return s // (NZ * NC), (s // NC) % NZ, s % NC


CORE_SWAP = [(s, s ^ 1) for s in range(SEQ)]
ZC_GROUPS = [[seq_of(y, z, c) for z in range(NZ) for c in range(NC)] for y in range(NY)]


def y_pairs(step):
    pairs = []
    for s in range(SEQ):
        y, z, c = coords_of(s)
        pairs.append((s, seq_of(y + step, z, c)))
    return pairs


def swap_cores(value):
    return lax.ppermute(value, "seq", CORE_SWAP)


def send_y(value, step):
    return lax.ppermute(value, "seq", y_pairs(step))


def send_x(value, step):
    return lax.ppermute(value, "mp", [(i, (i + step) % NX) for i in range(NX)])


def exchange(value, groups):
    return lax.all_to_all(value, "seq", 0, 0, axis_index_groups=groups, tiled=True)


def pick(value, index):
    return lax.dynamic_index_in_dim(value, index, 0, keepdims=False)


def gelu_tanh(values):
    return jax.nn.gelu(values, approximate=True)


def gather_by_y(column):
    return [column] + [send_y(column, step) for step in (1, 3, 2)]


STEPS = (0, 1, 3, 2)
CHUNK = 64


class Copies:
    def __init__(self, sems):
        self.sems, self.used = sems, 0

    def start(self, pairs):
        started = []
        for source, target in pairs:
            started.append(pltpu.make_async_copy(source, target, self.sems.at[self.used]))
            self.used += 1
            started[-1].start()
        return started


def wait(copies):
    for item in copies:
        item.wait()


def weight_pairs(at_ref, parts, full_ref):
    return [
        (part, full_ref.at[lax.rem(at_ref[1] + NY - step, NY)])
        for part, step in zip(parts, STEPS)
    ]


def norm_kernel(
    at_ref, own_ref, other_ref, normed_out, up_out, rms_out,
    pooled_ref, normed_ref, up_ref, rms_ref, sems,
):
    move = Copies(sems)
    rows, quarter = own_ref.shape[2:]
    places = []
    for half, part in enumerate((own_ref, other_ref)):
        for n, step in enumerate(STEPS):
            x = lax.rem(at_ref[0] + NX - step, NX)
            where = (
                pl.ds(half * rows, rows),
                pl.ds(pl.multiple_of(x * quarter, quarter), quarter),
            )
            places.append((part.at[n], where))
    pooled = move.start([(part.at[0], pooled_ref.at[where]) for part, where in places])
    ups = move.start([(part.at[1], up_ref.at[where]) for part, where in places])
    wait(pooled)

    def norm_rows(i, carry):
        at = pl.ds(pl.multiple_of(i * CHUNK, CHUNK), CHUNK)
        values = pooled_ref[at, :].astype(f32)
        rms = lax.rsqrt(jnp.mean(values * values, axis=1, keepdims=True) + epsilon)
        normed_ref[at, :] = (values * rms).astype(bf16)
        rms_ref[at, :] = jnp.broadcast_to(rms, (CHUNK, rms_ref.shape[1]))
        return carry

    lax.fori_loop(0, pooled_ref.shape[0] // CHUNK, norm_rows, 0)
    gone = move.start([(normed_ref, normed_out), (rms_ref, rms_out)])
    wait(ups)
    wait(gone + move.start([(up_ref, up_out)]))


def act_kernel(at_ref, *refs):
    parts, (normed_in, up_in, pre_out, out_out), refs = refs[:4], refs[4:8], refs[8:]
    normed_ref, up_ref, w_in_ref, pre_ref, act_ref, out_ref, sems = refs
    move = Copies(sems)
    first = move.start([(normed_in, normed_ref)] + weight_pairs(at_ref, parts, w_in_ref))
    second = move.start([(up_in, up_ref)])
    wait(first)
    rows, width = normed_ref.shape
    depth, hidden = w_in_ref.shape[1:]
    for n in range(0, hidden, 256):
        weight = w_in_ref[:, :, n : n + 256].reshape(width, 256)
        pre_ref[:, n : n + 256] = jnp.dot(normed_ref[...], weight, preferred_element_type=f32)
    gone = move.start([(pre_ref, pre_out)])

    def act_rows(i, carry):
        at = pl.ds(pl.multiple_of(i * CHUNK, CHUNK), CHUNK)
        act_ref[at, :] = gelu_tanh(pre_ref[at, :]).astype(bf16)
        return carry

    lax.fori_loop(0, rows // CHUNK, act_rows, 0)
    wait(second)
    for y in range(NY):
        part = lax.dot_general(
            up_ref[:, y * depth : (y + 1) * depth],
            act_ref[...],
            (((0,), (0,)), ((), ())),
            preferred_element_type=f32,
        ).astype(bf16)
        out_ref[y] = part.reshape(NZ * NC, 32, hidden)
        gone += move.start([(out_ref.at[y], out_out.at[:, pl.ds(y * 32, 32), :])])
    wait(gone)


GELU_K = math.sqrt(2.0 / math.pi)


def gelu_slope(v):
    square = v * v
    t = jnp.tanh(GELU_K * (v + 0.044715 * (square * v)))
    inner = GELU_K * (1.0 + 3 * 0.044715 * square)
    return 0.5 * (1.0 + t) + 0.5 * v * ((1.0 - t * t) * inner)


def grad_kernel(at_ref, *refs):
    parts, (normed_in, up_in, pre_in, rms_in), refs = refs[:4], refs[4:8], refs[8:]
    in_outs, (grad_out, row_out), refs = refs[:4], refs[4:6], refs[6:]
    normed_ref, up_ref, pre_ref, rms_ref, w_out_ref = refs[:5]
    proj_ref, grad_ref, row_ref, in_ref, sems = refs[5:]
    move = Copies(sems)
    first = move.start([(up_in, up_ref)] + weight_pairs(at_ref, parts, w_out_ref))
    second = move.start([(pre_in, pre_ref), (rms_in, rms_ref)])
    third = move.start([(normed_in, normed_ref)])
    wait(first)
    rows, width = normed_ref.shape
    depth, hidden = w_out_ref.shape[1:]
    for n in range(0, hidden, 256):
        weight = w_out_ref[:, :, n : n + 256].reshape(width, 256)
        proj_ref[:, n : n + 256] = jnp.dot(up_ref[...], weight, preferred_element_type=f32)
    wait(second)

    def grad_rows(i, carry):
        at = pl.ds(pl.multiple_of(i * CHUNK, CHUNK), CHUNK)
        pre = pre_ref[at, :]
        grad = (proj_ref[at, :] * gelu_slope(pre)).astype(bf16)
        grad_ref[at, :] = grad
        stat = jnp.sum(grad.astype(f32) * pre, axis=1, keepdims=True)
        row_ref[at, :] = jnp.broadcast_to(stat, (CHUNK, 128)) / rms_ref[at, :]
        return carry

    lax.fori_loop(0, rows // CHUNK, grad_rows, 0)
    wait(third)
    gone = move.start([(grad_ref, grad_out), (row_ref, row_out)])
    for n, step in enumerate(STEPS):
        y = lax.rem(at_ref[1] + step, NY)
        block = normed_ref[:, pl.ds(pl.multiple_of(y * depth, depth), depth)]
        in_ref[n] = lax.dot_general(
            block, grad_ref[...], (((0,), (0,)), ((), ())), preferred_element_type=f32
        ).astype(bf16)
        gone += move.start([(in_ref.at[n], in_outs[n])])
    wait(gone)


def normed_kernel(at_ref, *refs):
    parts, (grad_in, row_in, own_out, sent_out, stat_out), refs = refs[:4], refs[4:9], refs[9:]
    grad_ref, row_ref, w_in_ref, own_ref, sent_ref, sems = refs
    move = Copies(sems)
    copies = move.start(
        [(grad_in, grad_ref), (row_in, row_ref)] + weight_pairs(at_ref, parts, w_in_ref)
    )
    wait(copies)
    half = grad_ref.shape[0] // 2
    depth = w_in_ref.shape[1]
    width = NY * depth
    gone = move.start([(row_ref.at[pl.ds(0, half), :], stat_out)])
    for n in range(NY):
        part = lax.dot_general(
            grad_ref[...], w_in_ref[n], (((1,), (1,)), ((), ())), preferred_element_type=f32
        )
        own_ref[:, n * depth : (n + 1) * depth] = part[:half]
        sent_ref[:, n * depth : (n + 1) * depth] = part[half:].astype(bf16)
    stat = row_ref[half:, :]
    high = stat.astype(bf16).astype(f32)
    lane = lax.broadcasted_iota(jnp.int32, (half, 128), 1)
    low = jnp.where(lane == 1, stat - high, 0.0)
    sent_ref[:, width:] = jnp.where(lane == 0, high, low).astype(bf16)
    wait(gone + move.start([(own_ref, own_out), (sent_ref, sent_out)]))


def call(kernel, at, far, outs, scratch, n_copies, flops):
    outs = [jax.ShapeDtypeStruct(shape, dtype) for shape, dtype in outs]
    moved = sum(v.size * v.dtype.itemsize for v in [*far, *outs])
    return pl.pallas_call(
        kernel,
        out_shape=tuple(outs),
        in_specs=[pl.BlockSpec(memory_space=pltpu.SMEM)]
        + [pl.BlockSpec(memory_space=pl.ANY)] * len(far),
        out_specs=(pl.BlockSpec(memory_space=pltpu.HBM),) * len(outs),
        scratch_shapes=[pltpu.VMEM(shape, dtype) for shape, dtype in scratch]
        + [pltpu.SemaphoreType.DMA((n_copies,))],
        cost_estimate=pl.CostEstimate(flops=flops, bytes_accessed=moved, transcendentals=0),
    )(at, *far)


def reduce_sent(own, pieces):
    total = own.astype(f32)
    for piece, step in zip(pieces, STEPS[1:]):
        total = total + send_y(piece, step).astype(f32)
    return total


def reduce_by_y(pieces, y_idx):
    total = pick(pieces, y_idx).astype(f32)
    for step in (1, 3, 2):
        got = send_y(pick(pieces, (y_idx + step) % NY).astype(bf16), step)
        total = total + got.astype(f32)
    return total


def local(byte_acts, byte_grads, row_of_byte, w_in, w_out):
    quarter = byte_acts.shape[1]
    width = quarter * NX
    hidden = w_in.shape[1] // NC
    shard_idx = lax.axis_index("seq")
    x_idx = lax.axis_index("mp")
    y_idx = shard_idx // (NZ * NC)

    def spread(weight):
        halves = weight.reshape(1, 32, NC, hidden).swapaxes(1, 2)
        copies = jnp.broadcast_to(halves, (NZ, NC, 32, hidden)).reshape(NZ * NC, 32, hidden)
        return exchange(copies, ZC_GROUPS).reshape(NZ * NC * 32, hidden)

    in_column = spread(w_in)
    in_parts = gather_by_y(in_column)
    out_column = spread(w_out)
    out_parts = gather_by_y(out_column)

    local_row = row_of_byte - shard_idx * CAP
    leading = local_row < 0
    slot_idx = jnp.where(leading, CAP, local_row)
    one_hot = (jnp.arange(CAP + 1, dtype=jnp.int32)[:, None] == slot_idx[None, :]).astype(bf16)
    act_sums = jnp.dot(one_hot, byte_acts, preferred_element_type=f32)
    grad_sums = jnp.dot(one_hot, byte_grads, preferred_element_type=f32)
    byte_counts = jnp.sum(one_hot.astype(f32), axis=1)
    frag = jnp.stack(
        [act_sums[CAP], grad_sums[CAP], jnp.broadcast_to(byte_counts[CAP], (quarter,))]
    )
    own_count = jnp.max(jnp.where(leading, -1, local_row)) + 1
    frag = lax.ppermute(frag, "seq", [(s, s - 1) for s in range(1, SEQ)])
    last_mark = (jnp.arange(CAP, dtype=jnp.int32) == own_count - 1).astype(f32)
    act_total = act_sums[:CAP] + last_mark[:, None] * frag[0][None, :]
    grad_total = grad_sums[:CAP] + last_mark[:, None] * frag[1][None, :]
    row_lengths = byte_counts[:CAP] + last_mark * frag[2, 0]
    inv_length = 1.0 / jnp.maximum(row_lengths, 1.0)
    pooled = (act_total * inv_length[:, None]).astype(bf16)
    up_grad = grad_total.astype(bf16)

    rows = jnp.stack([pooled, up_grad])
    own_parts = [rows] + [send_x(rows, step) for step in (1, 3, 2)]
    own_parts = jnp.stack(own_parts)
    other_parts = swap_cores(own_parts)
    at = jnp.stack([x_idx, y_idx]).astype(jnp.int32)
    rows_all, depth = 2 * CAP, width // NY
    wide, thin = ((rows_all, width), bf16), ((rows_all, 128), f32)
    square, weight = ((rows_all, hidden), f32), ((NY, depth, hidden), bf16)
    normed, wide_up, wide_rms = call(
        norm_kernel,
        at,
        [own_parts, other_parts],
        [wide, wide, thin],
        [wide, wide, wide, thin],
        19,
        0,
    )
    product = 2 * rows_all * width * hidden
    pre_act, out_pieces = call(
        act_kernel,
        at,
        [*in_parts, normed, wide_up],
        [square, ((NZ * NC, NY * 32, hidden), bf16)],
        [wide, wide, weight, square, ((rows_all, hidden), bf16), ((NY, NZ * NC, 32, hidden), bf16)],
        11,
        2 * product,
    )
    out_rows = exchange(out_pieces, ZC_GROUPS)
    out_rows = jnp.sum(out_rows.astype(f32).reshape(NZ, NC, NY, 32, hidden), axis=0)
    grad_out = reduce_by_y(out_rows.swapaxes(0, 1), y_idx)
    hidden_rows = ((rows_all, hidden), bf16)
    *in_pieces, act_grad, row_stats = call(
        grad_kernel,
        at,
        [*out_parts, normed, wide_up, pre_act, wide_rms],
        [((depth, hidden), bf16)] * NY + [hidden_rows, thin],
        [wide, wide, square, thin, weight, square, hidden_rows, thin, weight],
        14,
        2 * product,
    )
    in_rows = reduce_sent(in_pieces[0], in_pieces[1:])
    in_rows = exchange(in_rows.astype(bf16).reshape(NZ * NC, 32, hidden), ZC_GROUPS)
    grad_in = jnp.sum(in_rows.astype(f32).reshape(NZ, NC, 32, hidden), axis=0)

    own_shape, sent_shape = ((CAP, width), f32), ((CAP, width + 128), bf16)
    own_part, sent, own_stat = call(
        normed_kernel,
        at,
        [*in_parts, act_grad, row_stats],
        [own_shape, sent_shape, ((CAP, 128), f32)],
        [hidden_rows, thin, weight, own_shape, sent_shape],
        9,
        product,
    )
    got = swap_cores(sent)
    got = got.astype(f32)
    chip_part = own_part + got[:, :width]
    chip_stat = own_stat[:, 0] + got[:, width] + got[:, width + 1]
    lane = jnp.arange(128)[None, :]
    stat_high = chip_stat.astype(bf16)
    stat_low = (chip_stat - stat_high.astype(f32)).astype(bf16)
    stat_cols = jnp.where(lane == 0, stat_high[:, None], stat_low[:, None])
    stat_cols = jnp.where(lane < 2, stat_cols, jnp.zeros((), bf16))
    normed_grad = lax.dynamic_slice_in_dim(chip_part, x_idx * quarter, quarter, 1)
    row_stat = chip_stat
    for step in (1, 3, 2):
        piece = lax.dynamic_slice_in_dim(
            chip_part, ((x_idx + step) % NX) * quarter, quarter, 1
        ).astype(bf16)
        piece = jnp.concatenate([piece, stat_cols], axis=1)
        got = send_x(piece, step)
        got = got.astype(f32)
        normed_grad = normed_grad + got[:, :quarter]
        row_stat = row_stat + got[:, quarter] + got[:, quarter + 1]
    row_stat = row_stat / width
    own_rms = wide_rms[:CAP, 0]
    pooled_grad = (
        up_grad.astype(f32)
        + own_rms[:, None] * normed_grad
        - pooled.astype(f32) * (own_rms**3 * row_stat)[:, None]
    ).astype(bf16)

    grad_spread = pooled_grad.astype(f32) * inv_length[:, None]
    last_spread = lax.dynamic_slice_in_dim(grad_spread, own_count - 1, 1, 0)
    tail_spread = lax.ppermute(last_spread, "seq", [(s, s + 1) for s in range(SEQ - 1)])
    grad_table = jnp.concatenate([grad_spread, tail_spread], axis=0)
    byte_act_grad = (byte_grads.astype(f32) + jnp.take(grad_table, slot_idx, axis=0)).astype(bf16)

    grad_scale = 1.0 / math.sqrt(SEQ * BAL)
    grad_in = grad_in.swapaxes(0, 1).reshape(32, NC * hidden) * grad_scale
    grad_out = grad_out.swapaxes(0, 1).reshape(32, NC * hidden) * grad_scale
    return (byte_act_grad, grad_in, grad_out)


def solution(mesh):
    in_specs = (P("seq", "mp"), P("seq", "mp"), P("seq"), P("seq", "mp"), P("seq", "mp"))
    out_specs = (P("seq", "mp"), P("seq", "mp"), P("seq", "mp"))

    return jax.shard_map(local, mesh=mesh, in_specs=in_specs, out_specs=out_specs, check_vma=False)
```
